32 devices in a mesh: outer: 1, inner: 32 (over z, y, x, core).
Axes of the slice: x: 2, y: 2, z: 4, core: 2. Of those that a mesh axis runs over, the one named last changes fastest.
Arguments:
- b_leaf: float32 [8192, 64], P(('outer', 'inner')), may hold values from -6 to 6
- b_sep: float32 [256, 64], P(('outer', 'inner')), may hold values from -6 to 6
- b_root: float32 [256, 64], P(('outer', 'inner')), may hold values from -6 to 6
- leaf_linv: float32 [8192, 256], P(('outer', 'inner')), as said below
- leaf_uinv: float32 [8192, 256], P(('outer', 'inner')), as said below
- leaf_lower: float32 [8192, 256], P(('outer', 'inner')), as said below
- leaf_upper: float32 [8192, 256], P(('outer', 'inner')), as said below
- sep_rows: int32 [32, 256], P(('outer', 'inner')), may hold values from 0 to 255, as said below
- sep_linv: float32 [256, 256], P(('outer', 'inner')), as said below
- sep_uinv: float32 [256, 256], P(('outer', 'inner')), as said below
- sep_lower: float32 [256, 256], P(None, ('outer', 'inner')), as said below
- sep_upper: float32 [256, 256], P(('outer', 'inner')), as said below
- root_linv: float32 [256, 256], P(('outer', 'inner')), as said below
- root_uinv: float32 [256, 256], P(('outer', 'inner')), as said below
- basis_leaf: float32 [8192, 512], P(('outer', 'inner')), as said below
- basis_sep: float32 [256, 512], P(('outer', 'inner')), as said below
- basis_root: float32 [256, 512], P(('outer', 'inner')), as said below
- g_blocks: float32 [32768, 128], P(('outer', 'inner')), may hold values from -0.25 to 0.25
- c_blocks: float32 [32768, 128], P(('outer', 'inner')), may hold values from -0.25 to 0.25
- block_cols: int32 [64, 4], P(('outer', 'inner')), may hold values from 0 to 1
Outputs:
- v_leaf: float32 [8192, 64], P(('outer', 'inner'))
- v_sep: float32 [256, 64], P(('outer', 'inner'))
- v_root: float32 [256, 64], P(('outer', 'inner'))
- coefficients: float32 [512, 64], replicated
- reduced_g: float32 [64, 64], replicated
- reduced_c: float32 [64, 64], replicated
The draws below stay inside these ranges and needn't reach their ends.
Inputs may be any that keep to these rules, and one draw needn't show every extreme that they name: `sep_rows`: each row holds 256 distinct numbers; every row names 0 and 255. `leaf_linv`: lower triangular in each diagonal block of the stack, nonzero diagonal. `leaf_uinv`: upper triangular in each diagonal block of the stack, nonzero diagonal. `sep_linv`: lower triangular in each block of 256 rows, nonzero diagonal. `sep_uinv`: upper triangular in each block of 256 rows, nonzero diagonal. `root_linv`: lower triangular, nonzero diagonal. `root_uinv`: upper triangular, nonzero diagonal. `leaf_lower`: entries of order one over the square root of 256. `leaf_upper`: entries of order one over the square root of 256. `sep_lower`: entries of order one over the square root of the number of its columns. `sep_upper`: entries of order one over the square root of 256. basis_leaf, basis_sep and basis_root stacked by rows form Q with Q^T Q = 8704 I up to float32 rounding. `basis_sep`: part of the stacked Q described with basis_leaf. `basis_root`: part of the stacked Q described with basis_leaf.
All inputs are finite; a program needn't handle non-finite values.
Results may differ from the reference program's by a relative error of at most 0.0003.
Values sent between devices are 32-bit elements; how exact they have to be, the bound alone decides.
No kernel may reach another device: no remote copies, remote signals or barrier semaphores. Data moves between devices by JAX's collectives and lax.ppermute only.
A program may use at most 64 MiB of HBM per device.

```python
import math
import jax
import jax.numpy as jnp
from jax import lax

P_SIZE = 64
BASIS = 512
NL = 256
SO_DEV = 8
SR_DEV = 8
KR = 256
BLK = 128
WID = 4
SO = 256
SR = 256
NBR = 2
N_OUTER = 1
N_INNER = 32
DEVICES = 32


def triangle_stack(key, stack_count, extent, is_lower):
    key_off, key_diag = jax.random.split(key)
    off_diag = jax.random.normal(key_off, (stack_count, extent, extent)) * 0.7 / math.sqrt(extent)
    diagonal_vals = jax.random.uniform(key_diag, (stack_count, extent), minval=0.5, maxval=1.5)
    row_ids = jnp.arange(extent)[:, None]
    col_ids = jnp.arange(extent)[None, :]
    if is_lower:
        keep = row_ids > col_ids
    else:
        keep = row_ids < col_ids
    matrix = jnp.where(keep[None], off_diag, 0.0) + diagonal_vals[:, :, None] * (row_ids == col_ids)[None].astype(jnp.float32)
    return matrix.reshape(stack_count * extent, extent).astype(jnp.float32)


def dense_draw(key, row_total, col_total, fan_in):
    values = jnp.clip(jax.random.normal(key, (row_total, col_total)), -6.0, 6.0)
    return (values / math.sqrt(fan_in)).astype(jnp.float32)


def draw_leaf_linv(key, part):
    return triangle_stack(jax.random.fold_in(key, 11), DEVICES, NL, True)


def draw_leaf_uinv(key, part):
    return triangle_stack(jax.random.fold_in(key, 12), DEVICES, NL, False)


def draw_sep_linv(key, part):
    return triangle_stack(jax.random.fold_in(key, 13), N_OUTER, SO, True)


def draw_sep_uinv(key, part):
    return triangle_stack(jax.random.fold_in(key, 14), N_OUTER, SO, False)


def draw_root_linv(key, part):
    return triangle_stack(jax.random.fold_in(key, 15), 1, SR, True)


def draw_root_uinv(key, part):
    return triangle_stack(jax.random.fold_in(key, 16), 1, SR, False)


def draw_sep_rows(key, part):
    row_keys = jax.random.split(jax.random.fold_in(key, 17), DEVICES)

    def draw_row(row_key):
        shuffled = jax.random.permutation(row_key, SO - 2)[:KR - 2].astype(jnp.int32) + 1
        return jnp.concatenate([jnp.zeros((1,), jnp.int32), shuffled, jnp.full((1,), SO - 1, jnp.int32)])
    return jax.vmap(draw_row)(row_keys)


def draw_b_leaf(key, part):
    return dense_draw(jax.random.fold_in(key, 18), DEVICES * NL, P_SIZE, 1)


def draw_b_sep(key, part):
    return dense_draw(jax.random.fold_in(key, 19), N_OUTER * SO, P_SIZE, 1)


def draw_b_root(key, part):
    return dense_draw(jax.random.fold_in(key, 20), SR, P_SIZE, 1)


def draw_leaf_lower(key, part):
    return dense_draw(jax.random.fold_in(key, 21), DEVICES * KR, NL, NL)


def draw_leaf_upper(key, part):
    return dense_draw(jax.random.fold_in(key, 22), DEVICES * NL, KR, KR)


def draw_sep_upper(key, part):
    return dense_draw(jax.random.fold_in(key, 23), N_OUTER * SO, SR, SR)


def draw_sep_lower(key, part):
    base_key = jax.random.fold_in(key, 24)
    values = dense_draw(base_key, SR, N_OUTER * SO, N_OUTER * SO)
    pairing = jax.random.permutation(jax.random.fold_in(base_key, 1), DEVICES).astype(jnp.int32)
    row_block = jnp.arange(SR, dtype=jnp.int32) // SR_DEV
    col_block = jnp.arange(N_OUTER * SO, dtype=jnp.int32) // SO_DEV
    paired = pairing[col_block][None, :] == row_block[:, None]
    return jnp.where(paired, 6.0 * values, values).astype(jnp.float32)


def solve_ports(key, part):
    highest = lax.Precision.HIGHEST
    b_leaf = draw_b_leaf(key, part)
    b_sep = draw_b_sep(key, part)
    b_root = draw_b_root(key, part)
    leaf_linv = draw_leaf_linv(key, part)
    leaf_uinv = draw_leaf_uinv(key, part)
    leaf_lower = draw_leaf_lower(key, part)
    leaf_upper = draw_leaf_upper(key, part)
    sep_rows = draw_sep_rows(key, part)
    sep_linv = draw_sep_linv(key, part)
    sep_uinv = draw_sep_uinv(key, part)
    sep_lower = draw_sep_lower(key, part)
    sep_upper = draw_sep_upper(key, part)
    root_linv = draw_root_linv(key, part)
    root_uinv = draw_root_uinv(key, part)
    y_leaf = jnp.einsum('dij,djp->dip', leaf_linv.reshape(DEVICES, NL, NL), b_leaf.reshape(DEVICES, NL, P_SIZE), precision=highest)
    contrib = jnp.einsum('dkj,djp->dkp', leaf_lower.reshape(DEVICES, KR, NL), y_leaf, precision=highest)
    group_of = (jnp.arange(DEVICES, dtype=jnp.int32) // N_INNER)[:, None]
    target = (group_of * SO + sep_rows).reshape(-1).astype(jnp.int32)
    t_sep = jax.ops.segment_sum(contrib.reshape(DEVICES * KR, P_SIZE), target, num_segments=N_OUTER * SO)
    r_sep = (b_sep - t_sep).reshape(N_OUTER, SO, P_SIZE)
    y_sep = jnp.einsum('gij,gjp->gip', sep_linv.reshape(N_OUTER, SO, SO), r_sep, precision=highest).reshape(N_OUTER * SO, P_SIZE)
    y_root = jnp.dot(root_linv, b_root - jnp.dot(sep_lower, y_sep, precision=highest), precision=highest)
    x_root = jnp.dot(root_uinv, y_root, precision=highest)
    z_sep = (y_sep - jnp.dot(sep_upper, x_root, precision=highest)).reshape(N_OUTER, SO, P_SIZE)
    x_sep = jnp.einsum('gij,gjp->gip', sep_uinv.reshape(N_OUTER, SO, SO), z_sep, precision=highest)
    coupled = x_sep[group_of, sep_rows]
    z_leaf = y_leaf - jnp.einsum('dik,dkp->dip', leaf_upper.reshape(DEVICES, NL, KR), coupled, precision=highest)
    x_leaf = jnp.einsum('dij,djp->dip', leaf_uinv.reshape(DEVICES, NL, NL), z_leaf, precision=highest).reshape(DEVICES * NL, P_SIZE)
    return jnp.concatenate([x_leaf, x_sep.reshape(N_OUTER * SO, P_SIZE), x_root], axis=0)


def orthonormal_basis(key, part):
    highest = lax.Precision.HIGHEST
    stacked = solve_ports(key, part)
    spread = jnp.sqrt(jnp.mean(stacked * stacked))
    key_noise, key_mix = jax.random.split(jax.random.fold_in(key, 30))
    total_rows = DEVICES * (NL + SO_DEV + SR_DEV)
    noise = jax.random.normal(key_noise, (total_rows, BASIS))
    mixing = jax.random.normal(key_mix, (P_SIZE, BASIS)) * (3.3 / math.sqrt(BASIS))
    raw = noise + jnp.dot(stacked / spread, mixing, precision=highest)
    for sweep in range(2):
        gram_now = jnp.dot(raw.T, raw, precision=highest)
        lower_now = jnp.linalg.cholesky(gram_now)
        raw = lax.linalg.triangular_solve(lower_now, raw, left_side=False, lower=True, transpose_a=True)
    return (raw * math.sqrt(total_rows)).astype(jnp.float32)


def draw_basis_leaf(key, part):
    return orthonormal_basis(key, part)[:DEVICES * NL]


def draw_basis_sep(key, part):
    return orthonormal_basis(key, part)[DEVICES * NL:DEVICES * NL + N_OUTER * SO]


def draw_basis_root(key, part):
    return orthonormal_basis(key, part)[DEVICES * NL + N_OUTER * SO:]


def with_ends(values, key, low, largest):
    longest = values.shape.index(max(values.shape))
    spots = []
    for shift in (0, 1):
        where = [jax.random.randint(jax.random.fold_in(key, axis), (), 0, length) for axis, length in enumerate(values.shape)]
        where[longest] = (where[longest] + shift) % values.shape[longest]
        spots.append(tuple(where))
    return values.at[spots[0]].set(low).at[spots[1]].set(largest)


def level_of(key, shape, pieces, least, largest):
    gain, own = 1.0, jax.random.fold_in(key, 6)
    for position, blocks in pieces:
        heights = jnp.exp(jax.random.uniform(jax.random.fold_in(own, position), (blocks,), jnp.float32, least / len(pieces), largest / len(pieces)))
        gain = gain * jnp.repeat(heights, shape[position] // blocks).reshape([-1 if axis == position else 1 for axis in range(len(shape))])
    return gain


def normal_values(key, dims, deviation, bound, shards=(), kind=jnp.bfloat16):
    factor_of = level_of(key, dims, shards, -0.22, 0.18) if shards else 1.0
    entries = jax.random.normal(key, dims, jnp.float32) * deviation * factor_of
    return jnp.minimum(jnp.maximum(entries, -bound), bound).astype(kind)


def setup_inputs(seed: int = 0) -> dict:
    key_of = jax.random.split(jax.random.key(seed), 21)
    b_leaf = draw_b_leaf(jax.random.fold_in(key_of[20], 71), 0)
    b_sep = draw_b_sep(jax.random.fold_in(key_of[20], 71), 0)
    b_root = draw_b_root(jax.random.fold_in(key_of[20], 71), 0)
    leaf_linv = draw_leaf_linv(jax.random.fold_in(key_of[20], 71), 0)
    leaf_uinv = draw_leaf_uinv(jax.random.fold_in(key_of[20], 71), 0)
    leaf_lower = draw_leaf_lower(jax.random.fold_in(key_of[20], 71), 0)
    leaf_upper = draw_leaf_upper(jax.random.fold_in(key_of[20], 71), 0)
    sep_rows = draw_sep_rows(jax.random.fold_in(key_of[20], 71), 0)
    sep_linv = draw_sep_linv(jax.random.fold_in(key_of[20], 71), 0)
    sep_uinv = draw_sep_uinv(jax.random.fold_in(key_of[20], 71), 0)
    sep_lower = draw_sep_lower(jax.random.fold_in(key_of[20], 71), 0)
    sep_upper = draw_sep_upper(jax.random.fold_in(key_of[20], 71), 0)
    root_linv = draw_root_linv(jax.random.fold_in(key_of[20], 71), 0)
    root_uinv = draw_root_uinv(jax.random.fold_in(key_of[20], 71), 0)
    basis_leaf = draw_basis_leaf(jax.random.fold_in(key_of[20], 71), 0)
    basis_sep = draw_basis_sep(jax.random.fold_in(key_of[20], 71), 0)
    basis_root = draw_basis_root(jax.random.fold_in(key_of[20], 71), 0)
    g_blocks = normal_values(key_of[17], (DEVICES * NL * WID, BLK), (BLK * WID) ** -0.5, 0.25, ((0, 32),), jnp.float32)
    c_blocks = normal_values(key_of[18], (DEVICES * NL * WID, BLK), (BLK * WID) ** -0.5, 0.25, ((0, 32),), jnp.float32)
    block_cols = with_ends(jax.random.randint(key_of[19], (DEVICES * NBR, WID), 0, NBR), jax.random.fold_in(key_of[19], 1), 0, NBR - 1).astype(jnp.int32)
    return dict(b_leaf=b_leaf, b_sep=b_sep, b_root=b_root, leaf_linv=leaf_linv, leaf_uinv=leaf_uinv, leaf_lower=leaf_lower, leaf_upper=leaf_upper, sep_rows=sep_rows, sep_linv=sep_linv, sep_uinv=sep_uinv, sep_lower=sep_lower, sep_upper=sep_upper, root_linv=root_linv, root_uinv=root_uinv, basis_leaf=basis_leaf, basis_sep=basis_sep, basis_root=basis_root, g_blocks=g_blocks, c_blocks=c_blocks, block_cols=block_cols)


def product_exact(left, right):
    return jnp.dot(left.astype(jnp.float32), right.astype(jnp.float32), precision=lax.Precision.HIGHEST, preferred_element_type=jnp.float32)

def reference(b_leaf, b_sep, b_root, leaf_linv, leaf_uinv, leaf_lower, leaf_upper, sep_rows, sep_linv, sep_uinv, sep_lower, sep_upper, root_linv, root_uinv, basis_leaf, basis_sep, basis_root, g_blocks, c_blocks, block_cols):
    highest = lax.Precision.HIGHEST
    devices_all = N_OUTER * N_INNER
    y_leaf = jnp.einsum('dij,djp->dip', leaf_linv.reshape(devices_all, NL, NL), b_leaf.reshape(devices_all, NL, P_SIZE), precision=highest)
    contrib = jnp.einsum('dkj,djp->dkp', leaf_lower.reshape(devices_all, KR, NL), y_leaf, precision=highest)
    group_of = (jnp.arange(devices_all, dtype=jnp.int32) // N_INNER)[:, None]
    target = (group_of * SO + sep_rows).reshape(-1).astype(jnp.int32)
    t_sep = jax.ops.segment_sum(contrib.reshape(devices_all * KR, P_SIZE), target, num_segments=N_OUTER * SO)
    r_sep = (b_sep - t_sep).reshape(N_OUTER, SO, P_SIZE)
    y_sep = jnp.einsum('gij,gjp->gip', sep_linv.reshape(N_OUTER, SO, SO), r_sep, precision=highest).reshape(N_OUTER * SO, P_SIZE)
    y_root = product_exact(root_linv, b_root - product_exact(sep_lower, y_sep))
    x_root = product_exact(root_uinv, y_root)
    z_sep = (y_sep - product_exact(sep_upper, x_root)).reshape(N_OUTER, SO, P_SIZE)
    x_sep = jnp.einsum('gij,gjp->gip', sep_uinv.reshape(N_OUTER, SO, SO), z_sep, precision=highest)
    coupled = x_sep[group_of, sep_rows]
    z_leaf = y_leaf - jnp.einsum('dik,dkp->dip', leaf_upper.reshape(devices_all, NL, KR), coupled, precision=highest)
    x_leaf = jnp.einsum('dij,djp->dip', leaf_uinv.reshape(devices_all, NL, NL), z_leaf, precision=highest).reshape(devices_all * NL, P_SIZE)
    x_sep = x_sep.reshape(N_OUTER * SO, P_SIZE)
    node_count = float(devices_all * (NL + SO_DEV + SR_DEV))
    pieces_x = (x_leaf, x_sep, x_root)
    pieces_q = (basis_leaf, basis_sep, basis_root)
    projected = sum((product_exact(basis.T, values) for basis, values in zip(pieces_q, pieces_x)))
    coefficients = projected / node_count
    cleaned = [values - product_exact(basis, coefficients) for basis, values in zip(pieces_q, pieces_x)]
    gram_matrix = sum((product_exact(piece_now.T, piece_now) for piece_now in cleaned)) / node_count
    chol_lower = jnp.linalg.cholesky(gram_matrix)
    inverse_lower = lax.linalg.triangular_solve(chol_lower, jnp.eye(P_SIZE, dtype=jnp.float32), left_side=True, lower=True)
    v_leaf = product_exact(cleaned[0], inverse_lower.T)
    v_sep = product_exact(cleaned[1], inverse_lower.T)
    v_root = product_exact(cleaned[2], inverse_lower.T)
    blocked = v_leaf.reshape(devices_all, NBR, BLK, P_SIZE)
    device_ids = jnp.arange(devices_all, dtype=jnp.int32)[:, None, None]
    picked = blocked[device_ids, block_cols.reshape(devices_all, NBR, WID)]
    g_image = jnp.einsum('drwij,drwjp->drip', g_blocks.reshape(devices_all, NBR, WID, BLK, BLK), picked, precision=highest)
    c_image = jnp.einsum('drwij,drwjp->drip', c_blocks.reshape(devices_all, NBR, WID, BLK, BLK), picked, precision=highest)
    reduced_g = jnp.einsum('drip,driq->pq', blocked, g_image, precision=highest) / node_count
    reduced_c = jnp.einsum('drip,driq->pq', blocked, c_image, precision=highest) / node_count
    return (v_leaf, v_sep, v_root, coefficients, reduced_g, reduced_c)
```

```python
import math

import jax
import jax.numpy as jnp
from jax import lax
from jax.sharding import PartitionSpec as P

LANES = 128
REPLICATE_BYTES = 4 << 20


def matmul_exact(left, right):
    return jnp.dot(left, right, precision=lax.Precision.HIGHEST, preferred_element_type=jnp.float32)


def contract_rows(left, right):
    return lax.dot_general(
        left,
        right,
        (((0,), (0,)), ((), ())),
        precision=lax.Precision.HIGHEST,
        preferred_element_type=jnp.float32,
    )


def axis_count(axes):
    return math.prod(lax.axis_size(axis) for axis in axes)


def exchange(blocks, axes):
    return lax.all_to_all(blocks, axes, 0, 0, tiled=True)


def gather_blocks(block, axes):
    count = axis_count(axes)
    return exchange(jnp.broadcast_to(block[None], (count,) + block.shape), axes)


def sum_over(arrays, axes):
    count = axis_count(axes)
    sizes = [array.size for array in arrays]
    flat = jnp.concatenate([array.reshape(-1) for array in arrays])
    depth = -(-flat.size // (count * LANES))
    flat = jnp.pad(flat, (0, count * depth * LANES - flat.size))
    part = exchange(flat.reshape(count, depth, LANES), axes).sum(axis=0)
    whole = gather_blocks(part, axes).reshape(-1)
    results, start = [], 0
    for array, size in zip(arrays, sizes):
        results.append(whole[start : start + size].reshape(array.shape))
        start += size
    return results


def gather_rows(rows, axes):
    count = axis_count(axes)
    bits = count.bit_length() - 1
    if count != 1 << bits:
        return gather_blocks(rows, axes).reshape((-1,) + rows.shape[1:])
    here = lax.axis_index(axes)
    held = rows
    for step, bit in enumerate(reversed(range(bits))):
        pairs = [(source, source ^ (1 << bit)) for source in range(count)]
        other = lax.ppermute(held, axes, pairs)
        upper = ((here >> bit) & 1) == 1
        first = jnp.where(upper, other, held)
        second = jnp.where(upper, held, other)
        held = jnp.stack([first, second], axis=step)
    return held.reshape((-1,) + rows.shape[1:])


def fold_triangles(lower, upper, row_start):
    row = row_start + lax.broadcasted_iota(jnp.int32, lower.shape, 0)
    col = lax.broadcasted_iota(jnp.int32, lower.shape, 1)
    diagonal = jnp.sum(jnp.where(row == col, lower, 0.0), axis=1, keepdims=True)
    return jnp.where(col < row, lower, upper), diagonal


def unfold_triangles(folded, diagonal):
    row = lax.broadcasted_iota(jnp.int32, folded.shape, 0)
    col = lax.broadcasted_iota(jnp.int32, folded.shape, 1)
    lower = jnp.where(col < row, folded, jnp.where(col == row, diagonal, 0.0))
    upper = jnp.where(col >= row, folded, 0.0)
    return lower, upper


def shards(
    b_leaf,
    b_sep,
    b_root,
    leaf_linv,
    leaf_uinv,
    leaf_lower,
    leaf_upper,
    sep_rows,
    sep_linv,
    sep_uinv,
    sep_lower,
    sep_upper,
    root_linv,
    root_uinv,
    basis_leaf,
    basis_sep,
    basis_root,
    g_blocks,
    c_blocks,
    block_cols,
):
    everyone = ("outer", "inner")
    group = ("inner",)
    ports = b_leaf.shape[1]
    sep_local = b_sep.shape[0]
    root_local = b_root.shape[0]
    sep_width = sep_linv.shape[1]
    root_width = root_linv.shape[1]
    in_group = lax.axis_index(group) * sep_local
    in_root = lax.axis_index(everyone) * root_local

    sep_folded, sep_diagonal = fold_triangles(sep_linv, sep_uinv, in_group)
    sep_packed = [sep_folded, jnp.broadcast_to(sep_diagonal, (sep_local, LANES))]
    replicate = 4 * 3 * root_width * root_width <= REPLICATE_BYTES and (
        lax.axis_size("outer") == 1 and sep_local == root_local
    )
    if replicate:
        root_folded, root_diagonal = fold_triangles(root_linv, root_uinv, in_root)
        packed = sep_packed + [
            sep_lower.T,
            sep_upper,
            root_folded,
            jnp.concatenate(
                [b_root, jnp.broadcast_to(root_diagonal, (root_local, ports))], axis=1
            ),
        ]
    else:
        packed = sep_packed
    gathered = gather_rows(jnp.concatenate(packed, axis=1), group)
    pieces, start = [], 0
    for piece in packed:
        pieces.append(gathered[:, start : start + piece.shape[1]])
        start += piece.shape[1]
    sep_lower_tri, sep_upper_tri = unfold_triangles(pieces[0], pieces[1][:, :1])

    selector = (sep_rows[0][:, None] == jnp.arange(sep_width, dtype=jnp.int32)[None, :]).astype(
        jnp.float32
    )
    y_leaf = matmul_exact(leaf_linv, b_leaf)
    contrib = matmul_exact(leaf_lower, y_leaf)
    placed = -contract_rows(selector, contrib)
    own = lax.dynamic_slice(placed, (in_group, 0), (sep_local, ports)) + b_sep
    placed = lax.dynamic_update_slice(placed, own, (in_group, 0))
    (sources,) = sum_over([placed], group)
    y_sep = matmul_exact(sep_lower_tri, sources)
    if replicate:
        lower_all = pieces[2].T
        upper_all = pieces[3]
        root_lower_tri, root_upper_tri = unfold_triangles(pieces[4], pieces[5][:, ports : ports + 1])
        b_root_all = pieces[5][:, :ports]
        y_root = matmul_exact(root_lower_tri, b_root_all - matmul_exact(lower_all, y_sep))
        x_root_all = matmul_exact(root_upper_tri, y_root)
        z_sep = y_sep - matmul_exact(upper_all, x_root_all)
        x_root = lax.dynamic_slice(x_root_all, (in_root, 0), (root_local, ports))
    else:
        count = axis_count(everyone)
        y_own = lax.dynamic_slice(y_sep, (in_group, 0), (sep_local, ports))
        partial = matmul_exact(sep_lower, y_own).reshape(count, root_local, ports)
        sources_root = b_root - exchange(partial, everyone).sum(axis=0)
        whole = gather_blocks(sources_root, everyone).reshape(root_width, ports)
        y_root = matmul_exact(root_linv, whole)
        whole = gather_blocks(y_root, everyone).reshape(root_width, ports)
        x_root = matmul_exact(root_uinv, whole)
        whole = gather_blocks(x_root, everyone).reshape(root_width, ports)
        z_own = y_own - matmul_exact(sep_upper, whole)
        z_sep = gather_blocks(z_own, group).reshape(sep_width, ports)
    x_sep_all = matmul_exact(sep_upper_tri, z_sep)
    x_sep = lax.dynamic_slice(x_sep_all, (in_group, 0), (sep_local, ports))
    coupled = matmul_exact(selector, x_sep_all)
    x_leaf = matmul_exact(leaf_uinv, y_leaf - matmul_exact(leaf_upper, coupled))

    node_count = float(axis_count(everyone) * (b_leaf.shape[0] + sep_local + root_local))
    pieces_x = (x_leaf, x_sep, x_root)
    pieces_q = (basis_leaf, basis_sep, basis_root)
    projected = sum(contract_rows(basis, values) for basis, values in zip(pieces_q, pieces_x))
    (coefficients,) = sum_over([projected], everyone)
    coefficients = coefficients / node_count
    cleaned = [
        values - matmul_exact(basis, coefficients) for basis, values in zip(pieces_q, pieces_x)
    ]
    local_gram = sum(contract_rows(piece, piece) for piece in cleaned)

    block_rows = block_cols.shape[0]
    stored = block_cols.shape[1]
    block_size = g_blocks.shape[1]
    blocked = cleaned[0].reshape(block_rows, block_size, ports)
    picked = (
        block_cols[:, :, None] == jnp.arange(block_rows, dtype=jnp.int32)[None, None, :]
    ).astype(jnp.float32)

    def reduced(blocks):
        tiles = blocks.reshape(block_rows, stored, block_size, block_size)
        dense = jnp.sum(
            picked[:, :, :, None, None] * tiles[:, :, None, :, :], axis=1
        )
        dense = dense.transpose(0, 2, 1, 3).reshape(block_rows * block_size, -1)
        return contract_rows(cleaned[0], matmul_exact(dense, cleaned[0]))

    gram_matrix, g_sum, c_sum = sum_over(
        [local_gram, reduced(g_blocks), reduced(c_blocks)], everyone
    )
    chol_lower = jnp.linalg.cholesky(gram_matrix / node_count)
    inverse_lower = lax.linalg.triangular_solve(
        chol_lower, jnp.eye(ports, dtype=jnp.float32), left_side=True, lower=True
    )
    v_leaf, v_sep, v_root = (matmul_exact(piece, inverse_lower.T) for piece in cleaned)
    g_out = matmul_exact(matmul_exact(inverse_lower, g_sum), inverse_lower.T) / node_count
    c_out = matmul_exact(matmul_exact(inverse_lower, c_sum), inverse_lower.T) / node_count
    return (v_leaf, v_sep, v_root, coefficients, g_out, c_out)


def solution(mesh):
    rows = P(("outer", "inner"), None)
    columns = P(None, ("outer", "inner"))
    return jax.shard_map(
        shards,
        mesh=mesh,
        in_specs=(rows,) * 10 + (columns,) + (rows,) * 9,
        out_specs=(rows, rows, rows, P(), P(), P()),
        check_vma=False,
    )
```

```python
import functools
import math

import jax
import jax.numpy as jnp
from jax import lax
from jax.experimental import pallas as pl
from jax.experimental.pallas import tpu as pltpu
from jax.sharding import PartitionSpec as P


LANES = 128
SUBLANES = 8
REPLICATE_BYTES = 4 << 20
VMEM_BYTES = 12 << 20
HOP_BITS = 2
EVERYONE = ("outer", "inner")
GROUP = ("inner",)
WHOLE = pl.BlockSpec(memory_space=pltpu.VMEM)
SCALAR = pl.BlockSpec(memory_space=pltpu.SMEM)


def contract(left, right, left_dim, right_dim, precision=lax.Precision.HIGHEST):
    return lax.dot_general(
        left,
        right,
        (((left_dim,), (right_dim,)), ((), ())),
        precision=precision,
        preferred_element_type=jnp.float32,
    )


def parts_of(value):
    high = value.astype(jnp.bfloat16)
    rest = value - high.astype(jnp.float32)
    middle = rest.astype(jnp.bfloat16)
    return high, middle, (rest - middle.astype(jnp.float32)).astype(jnp.bfloat16)


def dot_parts(left, right, right_dim):
    rows = left.shape[0]
    high, middle, low = parts_of(left)
    first, second, third = parts_of(right)
    three = contract(jnp.concatenate([high, middle, low], axis=0), first, 1, right_dim, None)
    two = contract(jnp.concatenate([high, middle], axis=0), second, 1, right_dim, None)
    one = contract(high, third, 1, right_dim, None)
    small = three[2 * rows :] + two[rows:] + one
    return three[:rows] + ((three[rows : 2 * rows] + two[:rows]) + small)


def dot_nn(left, right):
    return dot_parts(left, right, 0)


def dot_nt(left, right):
    return dot_parts(left, right, 1)


def dot_tn(left, right):
    return contract(left, right, 0, 0)


def axis_count(axes):
    return math.prod(lax.axis_size(axis) for axis in axes)


def shape_of(*dims):
    return jax.ShapeDtypeStruct(dims, jnp.float32)


def call(body, outs, operands, scalars=0, flops=0, limit=VMEM_BYTES):
    specs = [SCALAR] * scalars + [WHOLE] * (len(operands) - scalars)
    moved = sum(4 * operand.size for operand in operands) + sum(
        4 * math.prod(out.shape) for out in outs
    )
    return pl.pallas_call(
        body,
        out_shape=outs,
        in_specs=specs,
        out_specs=[WHOLE] * len(outs),
        compiler_params=pltpu.CompilerParams(vmem_limit_bytes=limit),
        cost_estimate=pl.CostEstimate(flops=flops, bytes_accessed=moved, transcendentals=0),
    )(*operands)


def iota(shape, dim):
    return lax.broadcasted_iota(jnp.int32, shape, dim)


def halves_up(wide):
    count = wide.shape[1] // LANES
    return jnp.concatenate(
        [wide[:, LANES * at : LANES * (at + 1)] for at in range(count)], axis=0
    )


def halves_down(tall, rows):
    count = tall.shape[0] // rows
    return jnp.concatenate([tall[rows * at : rows * (at + 1)] for at in range(count)], axis=1)


def exchange(blocks, axes):
    return lax.all_to_all(blocks, axes, 0, 0, tiled=True)


def gather_blocks(block, axes):
    count = axis_count(axes)
    return exchange(jnp.broadcast_to(block[None], (count,) + block.shape), axes)


def spread_kernel(scale, in_ref, out_ref):
    total = jnp.sum(in_ref[...], axis=0) * scale
    out_ref[...] = jnp.broadcast_to(total[None], out_ref.shape)


def sum_over(tall, axes, scale=1.0):
    count = axis_count(axes)
    size = tall.size
    depth = -(-size // (count * LANES))
    blocks = tall
    if size != count * depth * LANES:
        blocks = jnp.pad(tall.reshape(-1), (0, count * depth * LANES - size))
    blocks = blocks.reshape(count, depth, LANES)
    received = exchange(blocks, axes)
    (spread,) = call(
        functools.partial(spread_kernel, scale), [shape_of(count, depth, LANES)], [received]
    )
    whole = exchange(spread, axes)
    if size != count * depth * LANES:
        whole = whole.reshape(-1)[:size]
    return whole.reshape(tall.shape)


def swap_by_bits(blocks, position):
    size, bit = len(blocks), 0
    while 1 << bit < size:
        flip = ((position >> bit) & 1) == 1
        blocks = [
            jnp.where(flip, blocks[slot ^ (1 << bit)], blocks[slot]) for slot in range(size)
        ]
        bit += 1
    return blocks


def gather_rows(rows, axes):
    count = axis_count(axes)
    bits = count.bit_length() - 1
    here = lax.axis_index(axes)
    held = rows
    low = bits
    stage = 0
    while low > 1:
        width = min(HOP_BITS, low - 1)
        low -= width
        blocks = [held]
        for pattern in range(1, 1 << width):
            pairs = [(source, source ^ (pattern << low)) for source in range(count)]
            blocks.append(lax.ppermute(held, axes, pairs))
        held = jnp.stack(swap_by_bits(blocks, here >> low), axis=stage)
        stage += 1
    pairs = [(source, source ^ 1) for source in range(count)]
    other = lax.ppermute(held, axes, pairs)
    shape = (-1,) + rows.shape[1:]
    return held.reshape(shape), other.reshape(shape)


def leaf_kernel(at_ref, b_ref, linv_ref, lower_ref, rows_ref, b_sep_ref, y_ref, sources_ref):
    y_leaf = dot_nt(b_ref[...], linv_ref[...])
    y_ref[...] = y_leaf
    contrib = dot_nt(y_leaf, lower_ref[...])
    width = sources_ref.shape[0] // b_ref.shape[0] * LANES
    extent = rows_ref.shape[1]
    hits = iota((width, extent), 0) == rows_ref[...]
    placed = dot_nt(contrib, hits.astype(jnp.float32))
    own_rows = b_sep_ref.shape[0]
    own = iota((own_rows, width), 1) == iota((own_rows, width), 0) + at_ref[0]
    sources = dot_tn(b_sep_ref[...], own.astype(jnp.float32)) - placed
    sources_ref[...] = halves_up(sources)


def pack_kernel(
    at_ref, sl_ref, su_ref, lower_ref, upper_ref, rl_ref, ru_ref, b_root_ref, out_ref
):
    rows, width = sl_ref.shape
    own = iota((rows, width), 0) + at_ref[0]
    col = iota((rows, width), 1)

    def fold(lower, upper):
        diagonal = jnp.sum(jnp.where(col == own, lower, 0.0), axis=1, keepdims=True)
        return jnp.where(col < own, lower, upper), diagonal

    sep, sep_diagonal = fold(sl_ref[...], su_ref[...])
    root, root_diagonal = fold(rl_ref[...], ru_ref[...])
    out_ref[:, :width] = sep
    out_ref[:, width : 2 * width] = lower_ref[...]
    out_ref[:, 2 * width : 3 * width] = upper_ref[...]
    out_ref[:, 3 * width : 4 * width] = root
    ports = b_root_ref.shape[1]
    quarter = (LANES - ports) // 2
    out_ref[:, 4 * width :] = jnp.concatenate(
        [
            b_root_ref[...],
            jnp.broadcast_to(sep_diagonal, (rows, quarter)),
            jnp.broadcast_to(root_diagonal, (rows, quarter)),
        ],
        axis=1,
    )


def solve_kernel(
    at_ref,
    sources_ref,
    mine_ref,
    other_ref,
    y_ref,
    rows_ref,
    leaf_upper_ref,
    leaf_uinv_ref,
    q_leaf_ref,
    q_sep_ref,
    q_root_ref,
    x_ref,
    partial_ref,
):
    ports, extent = y_ref.shape
    own_rows = q_sep_ref.shape[0]
    width = 2 * mine_ref.shape[0]
    odd = (at_ref[0] // own_rows) % 2 == 1

    def piece(start, size):
        blocks = []
        for at in range(mine_ref.shape[0] // own_rows):
            mine = mine_ref[own_rows * at : own_rows * (at + 1), start : start + size]
            other = other_ref[own_rows * at : own_rows * (at + 1), start : start + size]
            blocks.append(jnp.where(odd, other, mine))
            blocks.append(jnp.where(odd, mine, other))
        return jnp.concatenate(blocks, axis=0)

    row = iota((width, width), 0)
    col = iota((width, width), 1)

    def unfold(folded, diagonal):
        lower = jnp.where(col < row, folded, jnp.where(col == row, diagonal, 0.0))
        return lower, jnp.where(col >= row, folded, 0.0)

    extra = piece(4 * width, LANES)
    quarter = (LANES - ports) // 2
    sep_l, sep_u = unfold(piece(0, width), extra[:, ports : ports + 1])
    root_l, root_u = unfold(
        piece(3 * width, width), extra[:, ports + quarter : ports + quarter + 1]
    )
    b_root = extra.T[:ports]
    sources = halves_down(sources_ref[...], ports)
    y_sep = dot_nt(sources, sep_l)
    y_root = dot_nt(b_root - dot_nn(y_sep, piece(width, width)), root_l)
    x_root = dot_nt(y_root, root_u)
    x_sep = dot_nt(y_sep - dot_nt(x_root, piece(2 * width, width)), sep_u)
    hits = (iota((width, extent), 0) == rows_ref[...]).astype(jnp.float32)
    coupled = dot_nn(x_sep, hits)
    x_leaf = dot_nt(y_ref[...] - dot_nt(coupled, leaf_upper_ref[...]), leaf_uinv_ref[...])
    own = iota((LANES, width), 1) - at_ref[0] == iota((LANES, width), 0)
    own = own & (iota((LANES, width), 0) < own_rows)
    shifted = iota((LANES, width), 1) - at_ref[0] == iota((LANES, width), 0) - own_rows
    shifted = shifted & (iota((LANES, width), 0) >= own_rows)
    shifted = shifted & (iota((LANES, width), 0) < 2 * own_rows)
    x_own = dot_nt(x_sep, own.astype(jnp.float32)) + dot_nt(x_root, shifted.astype(jnp.float32))
    x_ref[:, :extent] = x_leaf
    x_ref[:, extent:] = x_own
    q_own = jnp.concatenate([q_sep_ref[...], q_root_ref[...]], axis=0)
    partial = dot_nn(x_leaf, q_leaf_ref[...]) + dot_nn(x_own[:, : 2 * own_rows], q_own)
    partial_ref[...] = halves_up(partial)


def dense_kernel(cols_ref, g_ref, c_ref, g_out_ref, c_out_ref):
    block_rows, stored = cols_ref.shape
    size = g_ref.shape[1]
    for blocks_ref, out_ref in ((g_ref, g_out_ref), (c_ref, c_out_ref)):
        for row in range(block_rows):
            for col in range(block_rows):
                total = jnp.zeros((size, size), jnp.float32)
                for slot in range(stored):
                    start = (row * stored + slot) * size
                    block = blocks_ref[start : start + size, :]
                    total = total + jnp.where(cols_ref[row, slot] == col, block, 0.0)
                out_ref[size * row : size * (row + 1), size * col : size * (col + 1)] = total


def clean_kernel(
    coef_ref, x_ref, q_leaf_ref, q_sep_ref, q_root_ref, g_ref, c_ref, coef_out, clean_out, out_ref
):
    ports, extent = x_ref.shape[0], q_leaf_ref.shape[0]
    coef = halves_down(coef_ref[...], ports)
    coef_out[...] = coef
    leaf = x_ref[:, :extent] - dot_nt(coef, q_leaf_ref[...])
    q_own = jnp.concatenate([q_sep_ref[...], q_root_ref[...]], axis=0)
    pad = LANES - q_own.shape[0]
    q_own = jnp.concatenate([q_own, jnp.zeros((pad, q_own.shape[1]), jnp.float32)], axis=0)
    own = x_ref[:, extent:] - dot_nt(coef, q_own)
    clean_out[:, :extent] = leaf
    clean_out[:, extent:] = own
    g_image = dot_nt(leaf, g_ref[...])
    c_image = dot_nt(leaf, c_ref[...])
    products = dot_nt(leaf, jnp.concatenate([leaf, g_image, c_image], axis=0))
    gram = products[:, :ports] + dot_nt(own, own)
    out_ref[:ports, :] = jnp.concatenate([gram, products[:, ports : 2 * ports]], axis=1)
    out_ref[ports:, :] = jnp.concatenate(
        [products[:, 2 * ports :], jnp.zeros((ports, LANES - ports), jnp.float32)], axis=1
    )


def eliminate(tiles, offset, step):
    shape = tiles[0].shape
    rows = iota(shape, 0)
    tiles = list(tiles)

    def whole_row(tile, at):
        return jnp.broadcast_to(tile[at : at + 1, :], shape)

    def whole_col(tile, at):
        return jnp.broadcast_to(tile[:, at : at + 1], shape)

    for first in range(0, len(tiles) * SUBLANES, step):
        top, base = divmod(first, SUBLANES)
        pivots = [whole_row(tiles[top], base + t) for t in range(step)]
        columns = [
            [whole_col(tile, offset + first + t) for tile in tiles[top:]] for t in range(step)
        ]
        corner = [[whole_row(columns[u][0], base + t) for u in range(step)] for t in range(step)]
        factors = []
        for t in range(step):
            inverse = 1.0 / corner[t][t]
            for u in range(t + 1, step):
                ratio = corner[u][t] * inverse
                pivots[u] = pivots[u] - ratio * pivots[t]
                for v in range(t + 1, step):
                    corner[u][v] = corner[u][v] - ratio * corner[t][v]
            factor = [column * inverse for column in columns[t]]
            for v in range(t + 1, step):
                columns[v] = [c - f * corner[t][v] for c, f in zip(columns[v], factor)]
            factor[0] = jnp.where(rows > base + t, factor[0], 0.0)
            factors.append(factor)
        for at in range(top, len(tiles)):
            value = tiles[at]
            for t in range(step):
                value = value - factors[t][at - top] * pivots[t]
            tiles[at] = value
    return tiles


def tail_kernel(
    sums_ref, clean_ref, v_leaf_ref, v_sep_ref, v_root_ref, g_ref, c_ref
):
    ports = clean_ref.shape[0]
    extent = v_leaf_ref.shape[1]
    own_rows = v_sep_ref.shape[0]
    diagonal = iota((ports, ports), 0) == iota((ports, ports), 1)
    gram = sums_ref[:ports, :ports]
    joined = jnp.concatenate([jnp.where(diagonal, 1.0, 0.0), gram], axis=1)
    tiles = [joined[at : at + SUBLANES] for at in range(0, ports, SUBLANES)]
    joined = jnp.concatenate(eliminate(tiles, ports, SUBLANES), axis=0)
    pivots = jnp.sum(jnp.where(diagonal, joined[:, ports:], 0.0), axis=1, keepdims=True)
    inverse = joined[:, :ports] / jnp.sqrt(pivots)
    v_leaf_ref[...] = dot_nn(inverse, clean_ref[:, :extent])
    own = dot_nn(inverse, clean_ref[:, extent:]).T
    v_sep_ref[...] = own[:own_rows]
    v_root_ref[...] = own[own_rows : 2 * own_rows]
    g_sum = sums_ref[:ports, ports : 2 * ports]
    c_sum = sums_ref[ports:, :ports]
    g_ref[...] = dot_nt(dot_nn(inverse, g_sum), inverse)
    c_ref[...] = dot_nt(dot_nn(inverse, c_sum), inverse)


def solve_replicated(at, sources, b_root, factors, leaf, bases):
    sep_linv, sep_uinv, sep_lower, sep_upper, root_linv, root_uinv = factors
    ports, extent = leaf[0].shape
    sep_local, sep_width = sep_linv.shape
    basis = bases[0].shape[1]
    (packed,) = call(
        pack_kernel,
        [shape_of(sep_local, 4 * sep_width + LANES)],
        [at, sep_linv, sep_uinv, sep_lower.T, sep_upper, root_linv, root_uinv, b_root],
        scalars=1,
    )
    mine, other = gather_rows(packed, GROUP)
    return call(
        solve_kernel,
        [shape_of(ports, extent + LANES), shape_of(basis // LANES * ports, LANES)],
        [at, sources, mine, other, *leaf, *bases],
        scalars=1,
        flops=22 * extent * extent * ports,
    )


def solve_spread(at, sources, b_root, factors, leaf, bases):
    sep_linv, sep_uinv, sep_lower, sep_upper, root_linv, root_uinv = factors
    y_leaf, sep_rows, leaf_upper, leaf_uinv = leaf
    ports = y_leaf.shape[0]
    sep_local, sep_width = sep_linv.shape
    root_local, root_width = root_linv.shape
    row = iota((sep_local, sep_width), 0) + at[0]
    col = iota((sep_local, sep_width), 1)
    diagonal = jnp.sum(jnp.where(row == col, sep_linv, 0.0), axis=1, keepdims=True)
    folded = jnp.concatenate(
        [jnp.where(col < row, sep_linv, sep_uinv), jnp.broadcast_to(diagonal, (sep_local, LANES))],
        axis=1,
    )
    mine, other = gather_rows(folded, GROUP)
    odd = lax.axis_index(GROUP) % 2 == 1
    pair = jnp.stack(
        [
            block.reshape(-1, sep_local, folded.shape[1])
            for block in (jnp.where(odd, other, mine), jnp.where(odd, mine, other))
        ],
        axis=1,
    ).reshape(sep_width, -1)
    row = iota((sep_width, sep_width), 0)
    col = iota((sep_width, sep_width), 1)
    square = pair[:, :sep_width]
    sep_l = jnp.where(col < row, square, jnp.where(col == row, pair[:, sep_width:][:, :1], 0.0))
    sep_u = jnp.where(col >= row, square, 0.0)

    def own_rows(value):
        return lax.dynamic_slice(value, (at[0], 0), (sep_local, ports))

    y_sep = contract(sep_l, halves_down(sources, ports), 1, 1)
    count = axis_count(EVERYONE)
    update = contract(sep_lower, own_rows(y_sep), 1, 0).reshape(count, root_local, ports)
    held = b_root - exchange(update, EVERYONE).sum(axis=0)
    for factor in (root_linv, root_uinv):
        whole = gather_blocks(held, EVERYONE).reshape(root_width, ports)
        held = contract(factor, whole, 1, 0)
    x_root = held
    whole = gather_blocks(x_root, EVERYONE).reshape(root_width, ports)
    z_sep = own_rows(y_sep) - contract(sep_upper, whole, 1, 0)
    whole = gather_blocks(z_sep, GROUP).reshape(sep_width, ports)
    x_sep = contract(sep_u, whole, 1, 0)
    coupled = x_sep[sep_rows[0]]
    inner = y_leaf - contract(coupled, leaf_upper, 0, 1)
    x_leaf = contract(inner, leaf_uinv, 1, 1)
    own = jnp.concatenate([own_rows(x_sep), x_root], axis=0)
    partial = contract(x_leaf, bases[0], 1, 0) + contract(
        own, jnp.concatenate(bases[1:], axis=0), 0, 0
    )
    pad = jnp.zeros((ports, LANES - own.shape[0]), jnp.float32)
    return jnp.concatenate([x_leaf, own.T, pad], axis=1), halves_up(partial)


def shards(
    b_leaf,
    b_sep,
    b_root,
    leaf_linv,
    leaf_uinv,
    leaf_lower,
    leaf_upper,
    sep_rows,
    sep_linv,
    sep_uinv,
    sep_lower,
    sep_upper,
    root_linv,
    root_uinv,
    basis_leaf,
    basis_sep,
    basis_root,
    g_blocks,
    c_blocks,
    block_cols,
):
    extent, ports = b_leaf.shape
    sep_local = b_sep.shape[0]
    root_local = b_root.shape[0]
    sep_width = sep_linv.shape[1]
    basis = basis_leaf.shape[1]
    at = (lax.axis_index(GROUP) * sep_local).astype(jnp.int32).reshape(1)
    count = axis_count(EVERYONE)
    node_count = float(count * (extent + sep_local + root_local))
    square = extent * extent * ports

    y_leaf, sources = call(
        leaf_kernel,
        [shape_of(ports, extent), shape_of(sep_width // LANES * ports, LANES)],
        [at, b_leaf.T, leaf_linv, leaf_lower, sep_rows, b_sep],
        scalars=1,
        flops=6 * square,
        limit=None,
    )
    sources = sum_over(sources, GROUP)
    factors = (sep_linv, sep_uinv, sep_lower, sep_upper, root_linv, root_uinv)
    bases = (basis_leaf, basis_sep, basis_root)
    leaf = (y_leaf, sep_rows, leaf_upper, leaf_uinv)
    replicate = count == axis_count(GROUP) and sep_local == root_local
    if replicate and 4 * sep_width * (4 * sep_width + LANES) <= REPLICATE_BYTES:
        x_all, partial = solve_replicated(at, sources, b_root, factors, leaf, bases)
    else:
        x_all, partial = solve_spread(at, sources, b_root, factors, leaf, bases)
    coefficients = sum_over(partial, EVERYONE, 1.0 / node_count)
    g_dense, c_dense = call(
        dense_kernel, [shape_of(extent, extent)] * 2, [block_cols, g_blocks, c_blocks], scalars=1
    )
    coef_out, cleaned, products = call(
        clean_kernel,
        [shape_of(ports, basis), shape_of(ports, extent + LANES), shape_of(2 * ports, LANES)],
        [coefficients, x_all, basis_leaf, basis_sep, basis_root, g_dense, c_dense],
        flops=14 * square,
    )
    sums = sum_over(products, EVERYONE, 1.0 / node_count)
    v_leaf, v_sep, v_root, g_out, c_out = call(
        tail_kernel,
        [
            shape_of(ports, extent),
            shape_of(sep_local, ports),
            shape_of(root_local, ports),
            shape_of(ports, ports),
            shape_of(ports, ports),
        ],
        [sums, cleaned],
        flops=4 * square,
    )
    return (v_leaf.T, v_sep, v_root, coef_out.T, g_out, c_out)


def solution(mesh):
    rows = P(EVERYONE, None)
    columns = P(None, EVERYONE)
    return jax.shard_map(
        shards,
        mesh=mesh,
        in_specs=(rows,) * 10 + (columns,) + (rows,) * 9,
        out_specs=(rows, rows, rows, P(), P(), P()),
        check_vma=False,
    )
```

```python
import functools
import math

import jax
import jax.numpy as jnp
from jax import lax
from jax.experimental import pallas as pl
from jax.experimental.pallas import tpu as pltpu
from jax.sharding import PartitionSpec as P


LANES = 128
SUBLANES = 8
REPLICATE_BYTES = 4 << 20
VMEM_BYTES = 12 << 20
HOP_BITS = 2
HOP_DEVICES = 64
FIRST_UPWARD = True
EVERYONE = ("outer", "inner")
GROUP = ("inner",)
WHOLE = pl.BlockSpec(memory_space=pltpu.VMEM)
SCALAR = pl.BlockSpec(memory_space=pltpu.SMEM)


def contract(left, right, left_dim, right_dim, precision=lax.Precision.HIGHEST):
    return lax.dot_general(
        left,
        right,
        (((left_dim,), (right_dim,)), ((), ())),
        precision=precision,
        preferred_element_type=jnp.float32,
    )


def parts_of(value):
    high = value.astype(jnp.bfloat16)
    rest = value - high.astype(jnp.float32)
    middle = rest.astype(jnp.bfloat16)
    return high, middle, (rest - middle.astype(jnp.float32)).astype(jnp.bfloat16)


def dot_parts(left, right, right_dim):
    rows = left.shape[0]
    high, middle, low = parts_of(left)
    first, second, third = parts_of(right)
    three = contract(jnp.concatenate([high, middle, low], axis=0), first, 1, right_dim, None)
    two = contract(jnp.concatenate([high, middle], axis=0), second, 1, right_dim, None)
    one = contract(high, third, 1, right_dim, None)
    small = three[2 * rows :] + two[rows:] + one
    return three[:rows] + ((three[rows : 2 * rows] + two[:rows]) + small)


def dot_nn(left, right):
    return dot_parts(left, right, 0)


def dot_nt(left, right):
    return dot_parts(left, right, 1)


def dot_tn(left, right):
    return contract(left, right, 0, 0)


def axis_count(axes):
    return math.prod(lax.axis_size(axis) for axis in axes)


def shape_of(*dims):
    return jax.ShapeDtypeStruct(dims, jnp.float32)


def call(body, outs, operands, far=(), scalars=0, flops=0, limit=VMEM_BYTES):
    specs = [SCALAR] * scalars + [WHOLE] * (len(operands) - scalars)
    specs += [pl.BlockSpec(memory_space=pltpu.HBM)] * len(far)
    operands = [*operands, *far]
    moved = sum(4 * operand.size for operand in operands) + sum(
        4 * math.prod(out.shape) for out in outs
    )
    scratch = [pltpu.VMEM(operand.shape, operand.dtype) for operand in far]
    if far:
        scratch.append(pltpu.SemaphoreType.DMA((len(far),)))
    return pl.pallas_call(
        body,
        out_shape=outs,
        in_specs=specs,
        out_specs=[WHOLE] * len(outs),
        scratch_shapes=scratch,
        compiler_params=pltpu.CompilerParams(vmem_limit_bytes=limit),
        cost_estimate=pl.CostEstimate(flops=flops, bytes_accessed=moved, transcendentals=0),
    )(*operands)


def fetch(far, copies, semaphores):
    moves = [
        pltpu.make_async_copy(source, target, semaphores.at[at])
        for at, (source, target) in enumerate(zip(far, copies))
    ]
    for move in moves:
        move.start()

    def read(at):
        moves[at].wait()
        return copies[at][...]

    return read


def iota(shape, dim):
    return lax.broadcasted_iota(jnp.int32, shape, dim)


def halves_up(wide):
    count = wide.shape[1] // LANES
    return jnp.concatenate(
        [wide[:, LANES * at : LANES * (at + 1)] for at in range(count)], axis=0
    )


def halves_down(tall, rows):
    count = tall.shape[0] // rows
    return jnp.concatenate([tall[rows * at : rows * (at + 1)] for at in range(count)], axis=1)


def exchange(blocks, axes):
    return lax.all_to_all(blocks, axes, 0, 0, tiled=True)


def gather_blocks(block, axes):
    count = axis_count(axes)
    return exchange(jnp.broadcast_to(block[None], (count,) + block.shape), axes)


def spread_kernel(scale, in_ref, out_ref):
    total = jnp.sum(in_ref[...], axis=0) * scale
    out_ref[...] = jnp.broadcast_to(total[None], out_ref.shape)


def sum_over(tall, axes, scale=1.0):
    count = axis_count(axes)
    size = tall.size
    depth = -(-size // (count * LANES))
    blocks = tall
    if size != count * depth * LANES:
        blocks = jnp.pad(tall.reshape(-1), (0, count * depth * LANES - size))
    blocks = blocks.reshape(count, depth, LANES)
    received = exchange(blocks, axes)
    (spread,) = call(
        functools.partial(spread_kernel, scale), [shape_of(count, depth, LANES)], [received]
    )
    whole = exchange(spread, axes)
    if size != count * depth * LANES:
        whole = whole.reshape(-1)[:size]
    return whole.reshape(tall.shape)


def is_power_of_two(count):
    return count & (count - 1) == 0


def hop(value, axes, low, width):
    count = axis_count(axes)
    total = value
    for pattern in range(1, 1 << width):
        pairs = [(source, source ^ (pattern << low)) for source in range(count)]
        total = total + lax.ppermute(value, axes, pairs)
    return total


def halves_of(tall, axes):
    half = tall.shape[0] // 2
    odd = lax.axis_index(axes) % 2 == 1
    kept = jnp.where(odd, tall[half:], tall[:half])
    return kept, jnp.where(odd, tall[:half], tall[half:])


def swap_pair(value, axes):
    count = axis_count(axes)
    return lax.ppermute(value, axes, [(source, source ^ 1) for source in range(count)])


def join_halves(mine, other, axes):
    odd = lax.axis_index(axes) % 2 == 1
    return jnp.concatenate([jnp.where(odd, other, mine), jnp.where(odd, mine, other)])


def half_by_hops(kept, sent, axes, upward):
    total = kept + swap_pair(sent, axes)
    spans = spans_of(axis_count(axes).bit_length() - 1)
    if upward:
        spans.reverse()
    for low, width in spans:
        total = hop(total, axes, low, width)
    return total


def sum_by_hops(kept, sent, axes, scale, upward):
    total = half_by_hops(kept, sent, axes, upward) * scale
    return join_halves(total, swap_pair(total, axes), axes)


def by_hops(count):
    return is_power_of_two(count) and 1 < count <= HOP_DEVICES


def sum_all(tall, axes, scale, upward):
    if by_hops(axis_count(axes)) and tall.shape[0] % (2 * SUBLANES) == 0:
        return sum_by_hops(*halves_of(tall, axes), axes, scale, upward)
    return sum_over(tall, axes, scale)


def swap_by_bits(blocks, position):
    size, bit = len(blocks), 0
    while 1 << bit < size:
        flip = ((position >> bit) & 1) == 1
        blocks = [
            jnp.where(flip, blocks[slot ^ (1 << bit)], blocks[slot]) for slot in range(size)
        ]
        bit += 1
    return blocks


def spans_of(bits):
    spans, low = [], bits
    while low > 1:
        width = min(HOP_BITS, low - 1)
        low -= width
        spans.append((low, width))
    return spans


def gather_rows(rows, axes):
    count = axis_count(axes)
    here = lax.axis_index(axes)
    held = rows
    places, size = [0], 1
    spans = spans_of(count.bit_length() - 1)
    for low, width in spans:
        blocks = [held]
        for pattern in range(1, 1 << width):
            pairs = [(source, source ^ (pattern << low)) for source in range(count)]
            blocks.append(lax.ppermute(held, axes, pairs))
        held = jnp.concatenate(swap_by_bits(blocks, here >> low))
        places = [digit * size + place for place in places for digit in range(1 << width)]
        size <<= width
    return held, swap_pair(held, axes), places


def leaf_kernel(count, at_ref, *refs):
    far, (y_ref, kept_ref, sent_ref, *packed_ref) = refs[:count], refs[count : -count - 1]
    read = fetch(far, refs[-count - 1 : -1], refs[-1])
    b_leaf, linv = read(0), read(1)
    y_leaf = dot_nt(b_leaf, linv)
    y_ref[...] = y_leaf
    contrib = dot_nt(y_leaf, read(2))
    rows = read(3)
    b_sep = read(4)
    extent = rows.shape[1]
    width = 2 * kept_ref.shape[0] // b_leaf.shape[0] * LANES
    hits = iota((width, extent), 0) == rows
    placed = dot_nt(contrib, hits.astype(jnp.float32))
    own_rows = b_sep.shape[0]
    own = iota((own_rows, width), 1) == iota((own_rows, width), 0) + at_ref[0]
    tall = halves_up(dot_tn(b_sep, own.astype(jnp.float32)) - placed)
    half = kept_ref.shape[0]
    odd = (at_ref[0] // own_rows) % 2 == 1
    kept_ref[...] = jnp.where(odd, tall[half:], tall[:half])
    sent_ref[...] = jnp.where(odd, tall[:half], tall[half:])
    if packed_ref:
        pack_rows(at_ref[0], [read(at) for at in range(5, count)], packed_ref[0])


def pack_rows(at, values, out_ref):
    sep_l, sep_u, lower, upper, root_l, root_u, b_root = values
    rows, width = sep_l.shape
    own = iota((rows, width), 0) + at
    col = iota((rows, width), 1)

    def fold(lower, upper):
        diagonal = jnp.sum(jnp.where(col == own, lower, 0.0), axis=1, keepdims=True)
        return jnp.where(col < own, lower, upper), diagonal

    sep, sep_diagonal = fold(sep_l, sep_u)
    root, root_diagonal = fold(root_l, root_u)
    quarter = (LANES - b_root.shape[1]) // 2
    extra = jnp.concatenate(
        [
            b_root,
            jnp.broadcast_to(sep_diagonal, (rows, quarter)),
            jnp.broadcast_to(root_diagonal, (rows, quarter)),
        ],
        axis=1,
    )
    out_ref[...] = halves_up(jnp.concatenate([sep, lower, upper, root, extra], axis=1))


def solve_kernel(
    places,
    at_ref,
    half_ref,
    pair_ref,
    mine_ref,
    other_ref,
    y_ref,
    rows_ref,
    leaf_upper_ref,
    leaf_uinv_ref,
    q_leaf_ref,
    q_sep_ref,
    q_root_ref,
    x_ref,
    partial_ref,
):
    ports, extent = y_ref.shape
    own_rows = SUBLANES
    width = 2 * len(places) * own_rows
    tall = mine_ref.shape[0] // len(places)
    odd = (at_ref[0] // own_rows) % 2 == 1

    def ordered(mine, other):
        return jnp.where(odd, other, mine), jnp.where(odd, mine, other)

    def piece(first, size):
        strips = []
        for lane in range(first // LANES, (first + size) // LANES):
            blocks = []
            for place in places:
                start = place * tall + lane * own_rows
                rows = slice(start, start + own_rows)
                blocks.extend(ordered(mine_ref[rows], other_ref[rows]))
            strips.append(jnp.concatenate(blocks, axis=0))
        return jnp.concatenate(strips, axis=1)

    row = iota((width, width), 0)
    col = iota((width, width), 1)

    def unfold(folded, diagonal):
        lower = jnp.where(col < row, folded, jnp.where(col == row, diagonal, 0.0))
        return lower, jnp.where(col >= row, folded, 0.0)

    extra = piece(4 * width, LANES)
    quarter = (LANES - ports) // 2
    sep_l, sep_u = unfold(piece(0, width), extra[:, ports : ports + 1])
    root_l, root_u = unfold(
        piece(3 * width, width), extra[:, ports + quarter : ports + quarter + 1]
    )
    b_root = extra.T[:ports]
    sources = halves_down(jnp.concatenate(ordered(half_ref[...], pair_ref[...]), axis=0), ports)
    y_sep = dot_nt(sources, sep_l)
    y_root = dot_nt(b_root - dot_nn(y_sep, piece(width, width)), root_l)
    x_root = dot_nt(y_root, root_u)
    x_sep = dot_nt(y_sep - dot_nt(x_root, piece(2 * width, width)), sep_u)
    hits = (iota((width, extent), 0) == rows_ref[...]).astype(jnp.float32)
    coupled = dot_nn(x_sep, hits)
    x_leaf = dot_nt(y_ref[...] - dot_nt(coupled, leaf_upper_ref[...]), leaf_uinv_ref[...])
    own = iota((LANES, width), 1) - at_ref[0] == iota((LANES, width), 0)
    own = own & (iota((LANES, width), 0) < own_rows)
    shifted = iota((LANES, width), 1) - at_ref[0] == iota((LANES, width), 0) - own_rows
    shifted = shifted & (iota((LANES, width), 0) >= own_rows)
    shifted = shifted & (iota((LANES, width), 0) < 2 * own_rows)
    x_own = dot_nt(x_sep, own.astype(jnp.float32)) + dot_nt(x_root, shifted.astype(jnp.float32))
    x_ref[:, :extent] = x_leaf
    x_ref[:, extent:] = x_own
    q_own = jnp.concatenate([q_sep_ref[...], q_root_ref[...]], axis=0)
    partial = dot_nn(x_leaf, q_leaf_ref[...]) + dot_nn(x_own[:, : 2 * own_rows], q_own)
    partial_ref[...] = halves_up(partial)


def dense_kernel(cols_ref, g_ref, c_ref, g_out_ref, c_out_ref):
    block_rows, stored = cols_ref.shape
    size = g_ref.shape[1]
    for blocks_ref, out_ref in ((g_ref, g_out_ref), (c_ref, c_out_ref)):
        for row in range(block_rows):
            for col in range(block_rows):
                total = jnp.zeros((size, size), jnp.float32)
                for slot in range(stored):
                    start = (row * stored + slot) * size
                    block = blocks_ref[start : start + size, :]
                    total = total + jnp.where(cols_ref[row, slot] == col, block, 0.0)
                out_ref[size * row : size * (row + 1), size * col : size * (col + 1)] = total


def clean_kernel(
    coef_ref, x_ref, q_leaf_ref, q_sep_ref, q_root_ref, g_ref, c_ref, coef_out, clean_out, out_ref
):
    ports, extent = x_ref.shape[0], q_leaf_ref.shape[0]
    coef = halves_down(coef_ref[...], ports)
    coef_out[...] = coef
    leaf = x_ref[:, :extent] - dot_nt(coef, q_leaf_ref[...])
    q_own = jnp.concatenate([q_sep_ref[...], q_root_ref[...]], axis=0)
    pad = LANES - q_own.shape[0]
    q_own = jnp.concatenate([q_own, jnp.zeros((pad, q_own.shape[1]), jnp.float32)], axis=0)
    own = x_ref[:, extent:] - dot_nt(coef, q_own)
    clean_out[:, :extent] = leaf
    clean_out[:, extent:] = own
    g_image = dot_nt(leaf, g_ref[...])
    c_image = dot_nt(leaf, c_ref[...])
    products = dot_nt(leaf, jnp.concatenate([leaf, g_image, c_image], axis=0))
    gram = products[:, :ports] + dot_nt(own, own)
    out_ref[:ports, :] = jnp.concatenate([gram, products[:, ports : 2 * ports]], axis=1)
    out_ref[ports:, :] = jnp.concatenate(
        [products[:, 2 * ports :], jnp.zeros((ports, LANES - ports), jnp.float32)], axis=1
    )


def eliminate(tiles, offset, step):
    shape = tiles[0].shape
    rows = iota(shape, 0)
    tiles = list(tiles)

    def whole_row(tile, at):
        return jnp.broadcast_to(tile[at : at + 1, :], shape)

    def whole_col(tile, at):
        return jnp.broadcast_to(tile[:, at : at + 1], shape)

    for first in range(0, len(tiles) * SUBLANES, step):
        top, base = divmod(first, SUBLANES)
        pivots = [whole_row(tiles[top], base + t) for t in range(step)]
        columns = [
            [whole_col(tile, offset + first + t) for tile in tiles[top:]] for t in range(step)
        ]
        corner = [[whole_row(columns[u][0], base + t) for u in range(step)] for t in range(step)]
        factors = []
        for t in range(step):
            inverse = 1.0 / corner[t][t]
            for u in range(t + 1, step):
                ratio = corner[u][t] * inverse
                pivots[u] = pivots[u] - ratio * pivots[t]
                for v in range(t + 1, step):
                    corner[u][v] = corner[u][v] - ratio * corner[t][v]
            factor = [column * inverse for column in columns[t]]
            for v in range(t + 1, step):
                columns[v] = [c - f * corner[t][v] for c, f in zip(columns[v], factor)]
            factor[0] = jnp.where(rows > base + t, factor[0], 0.0)
            factors.append(factor)
        for at in range(top, len(tiles)):
            value = tiles[at]
            for t in range(step):
                value = value - factors[t][at - top] * pivots[t]
            tiles[at] = value
    return tiles


def tail_kernel(
    sums_ref, clean_ref, v_leaf_ref, v_sep_ref, v_root_ref, g_ref, c_ref
):
    ports = clean_ref.shape[0]
    extent = v_leaf_ref.shape[1]
    own_rows = v_sep_ref.shape[0]
    diagonal = iota((ports, ports), 0) == iota((ports, ports), 1)
    gram = sums_ref[:ports, :ports]
    joined = jnp.concatenate([jnp.where(diagonal, 1.0, 0.0), gram], axis=1)
    tiles = [joined[at : at + SUBLANES] for at in range(0, ports, SUBLANES)]
    joined = jnp.concatenate(eliminate(tiles, ports, SUBLANES), axis=0)
    pivots = jnp.sum(jnp.where(diagonal, joined[:, ports:], 0.0), axis=1, keepdims=True)
    inverse = joined[:, :ports] / jnp.sqrt(pivots)
    v_leaf_ref[...] = dot_nn(inverse, clean_ref[:, :extent])
    own = dot_nn(inverse, clean_ref[:, extent:]).T
    v_sep_ref[...] = own[:own_rows]
    v_root_ref[...] = own[own_rows : 2 * own_rows]
    g_sum = sums_ref[:ports, ports : 2 * ports]
    c_sum = sums_ref[ports:, :ports]
    g_ref[...] = dot_nt(dot_nn(inverse, g_sum), inverse)
    c_ref[...] = dot_nt(dot_nn(inverse, c_sum), inverse)


def solve_replicated(at, kept, sent, packed, y_leaf, late):
    ports, extent = y_leaf.shape
    basis = late[-1].shape[1]
    mine, other, places = gather_rows(packed, GROUP)
    half = half_by_hops(kept, sent, GROUP, FIRST_UPWARD)
    pair = swap_pair(half, GROUP)
    return call(
        functools.partial(solve_kernel, places),
        [shape_of(ports, extent + LANES), shape_of(basis // LANES * ports, LANES)],
        [at, half, pair, mine, other, y_leaf, *late],
        scalars=1,
        flops=22 * extent * extent * ports,
    )


def solve_spread(at, sources, b_root, factors, leaf, bases):
    sep_linv, sep_uinv, sep_lower, sep_upper, root_linv, root_uinv = factors
    y_leaf, sep_rows, leaf_upper, leaf_uinv = leaf
    ports = y_leaf.shape[0]
    sep_local, sep_width = sep_linv.shape
    root_local, root_width = root_linv.shape
    row = iota((sep_local, sep_width), 0) + at[0]
    col = iota((sep_local, sep_width), 1)
    diagonal = jnp.sum(jnp.where(row == col, sep_linv, 0.0), axis=1, keepdims=True)
    folded = jnp.concatenate(
        [jnp.where(col < row, sep_linv, sep_uinv), jnp.broadcast_to(diagonal, (sep_local, LANES))],
        axis=1,
    )
    pair = gather_blocks(folded, GROUP).reshape(sep_width, -1)
    row = iota((sep_width, sep_width), 0)
    col = iota((sep_width, sep_width), 1)
    square = pair[:, :sep_width]
    sep_l = jnp.where(col < row, square, jnp.where(col == row, pair[:, sep_width:][:, :1], 0.0))
    sep_u = jnp.where(col >= row, square, 0.0)

    def own_rows(value):
        return lax.dynamic_slice(value, (at[0], 0), (sep_local, ports))

    y_sep = contract(sep_l, halves_down(sources, ports), 1, 1)
    count = axis_count(EVERYONE)
    update = contract(sep_lower, own_rows(y_sep), 1, 0).reshape(count, root_local, ports)
    held = b_root - exchange(update, EVERYONE).sum(axis=0)
    for factor in (root_linv, root_uinv):
        whole = gather_blocks(held, EVERYONE).reshape(root_width, ports)
        held = contract(factor, whole, 1, 0)
    x_root = held
    whole = gather_blocks(x_root, EVERYONE).reshape(root_width, ports)
    z_sep = own_rows(y_sep) - contract(sep_upper, whole, 1, 0)
    whole = gather_blocks(z_sep, GROUP).reshape(sep_width, ports)
    x_sep = contract(sep_u, whole, 1, 0)
    coupled = x_sep[sep_rows[0]]
    inner = y_leaf - contract(coupled, leaf_upper, 0, 1)
    x_leaf = contract(inner, leaf_uinv, 1, 1)
    own = jnp.concatenate([own_rows(x_sep), x_root], axis=0)
    partial = contract(x_leaf, bases[0], 1, 0) + contract(
        own, jnp.concatenate(bases[1:], axis=0), 0, 0
    )
    pad = jnp.zeros((ports, LANES - own.shape[0]), jnp.float32)
    return jnp.concatenate([x_leaf, own.T, pad], axis=1), halves_up(partial)


def shards(
    b_leaf,
    b_sep,
    b_root,
    leaf_linv,
    leaf_uinv,
    leaf_lower,
    leaf_upper,
    sep_rows,
    sep_linv,
    sep_uinv,
    sep_lower,
    sep_upper,
    root_linv,
    root_uinv,
    basis_leaf,
    basis_sep,
    basis_root,
    g_blocks,
    c_blocks,
    block_cols,
):
    extent, ports = b_leaf.shape
    sep_local = b_sep.shape[0]
    root_local = b_root.shape[0]
    sep_width = sep_linv.shape[1]
    basis = basis_leaf.shape[1]
    at = (lax.axis_index(GROUP) * sep_local).astype(jnp.int32).reshape(1)
    count = axis_count(EVERYONE)
    node_count = float(count * (extent + sep_local + root_local))
    square = extent * extent * ports

    factors = (sep_linv, sep_uinv, sep_lower, sep_upper, root_linv, root_uinv)
    bases = (basis_leaf, basis_sep, basis_root)
    replicate = (
        count == axis_count(GROUP)
        and sep_local == root_local == SUBLANES
        and by_hops(count)
        and 4 * sep_width * (4 * sep_width + LANES) <= REPLICATE_BYTES
    )
    tall = sep_width // LANES * ports
    outs = [shape_of(ports, extent), shape_of(tall // 2, LANES), shape_of(tall // 2, LANES)]
    far = [b_leaf.T, leaf_linv, leaf_lower, sep_rows, b_sep]
    if replicate:
        outs.append(shape_of((4 * sep_width // LANES + 1) * sep_local, LANES))
        far += [sep_linv, sep_uinv, sep_lower.T, sep_upper, root_linv, root_uinv, b_root]
    y_leaf, kept, sent, *packed = call(
        functools.partial(leaf_kernel, len(far)),
        outs,
        [at],
        far=far,
        scalars=1,
        flops=6 * square,
        limit=None,
    )
    if replicate:
        late = [sep_rows, leaf_upper, leaf_uinv, *bases]
        x_all, partial = solve_replicated(at, kept, sent, *packed, y_leaf, late)
    else:
        if by_hops(axis_count(GROUP)):
            sources = sum_by_hops(kept, sent, GROUP, 1.0, False)
        else:
            sources = sum_over(join_halves(kept, sent, GROUP), GROUP)
        leaf = (y_leaf, sep_rows, leaf_upper, leaf_uinv)
        x_all, partial = solve_spread(at, sources, b_root, factors, leaf, bases)
    coefficients = sum_all(partial, EVERYONE, 1.0 / node_count, True)
    g_dense, c_dense = call(
        dense_kernel, [shape_of(extent, extent)] * 2, [block_cols, g_blocks, c_blocks], scalars=1
    )
    coef_out, cleaned, products = call(
        clean_kernel,
        [shape_of(ports, basis), shape_of(ports, extent + LANES), shape_of(2 * ports, LANES)],
        [coefficients, x_all, basis_leaf, basis_sep, basis_root, g_dense, c_dense],
        flops=14 * square,
    )
    sums = sum_all(products, EVERYONE, 1.0 / node_count, False)
    v_leaf, v_sep, v_root, g_out, c_out = call(
        tail_kernel,
        [
            shape_of(ports, extent),
            shape_of(sep_local, ports),
            shape_of(root_local, ports),
            shape_of(ports, ports),
            shape_of(ports, ports),
        ],
        [sums, cleaned],
        flops=4 * square,
    )
    return (v_leaf.T, v_sep, v_root, coef_out.T, g_out, c_out)


def solution(mesh):
    rows = P(EVERYONE, None)
    columns = P(None, EVERYONE)
    return jax.shard_map(
        shards,
        mesh=mesh,
        in_specs=(rows,) * 10 + (columns,) + (rows,) * 9,
        out_specs=(rows, rows, rows, P(), P(), P()),
        check_vma=False,
    )
```

```python
import functools
import math

import jax
import jax.numpy as jnp
from jax import lax
from jax.experimental import pallas as pl
from jax.experimental.pallas import tpu as pltpu
from jax.sharding import PartitionSpec as P


LANES = 128
SUBLANES = 8
REPLICATE_BYTES = 4 << 20
VMEM_BYTES = 12 << 20
HOP_BITS = 2
HOP_DEVICES = 64
FIRST_UPWARD = True
EVERYONE = ("outer", "inner")
GROUP = ("inner",)
WHOLE = pl.BlockSpec(memory_space=pltpu.VMEM)
SCALAR = pl.BlockSpec(memory_space=pltpu.SMEM)


def contract(left, right, left_dim, right_dim, precision=lax.Precision.HIGHEST):
    return lax.dot_general(
        left,
        right,
        (((left_dim,), (right_dim,)), ((), ())),
        precision=precision,
        preferred_element_type=jnp.float32,
    )


def parts_of(value):
    high = value.astype(jnp.bfloat16)
    rest = value - high.astype(jnp.float32)
    middle = rest.astype(jnp.bfloat16)
    return high, middle, (rest - middle.astype(jnp.float32)).astype(jnp.bfloat16)


def dot_parts(left, right, right_dim):
    rows = left.shape[0]
    high, middle, low = parts_of(left)
    first, second, third = parts_of(right)
    three = contract(jnp.concatenate([high, middle, low], axis=0), first, 1, right_dim, None)
    two = contract(jnp.concatenate([high, middle], axis=0), second, 1, right_dim, None)
    one = contract(high, third, 1, right_dim, None)
    small = three[2 * rows :] + two[rows:] + one
    return three[:rows] + ((three[rows : 2 * rows] + two[:rows]) + small)


def dot_nn(left, right):
    return dot_parts(left, right, 0)


def dot_nt(left, right):
    return dot_parts(left, right, 1)


def dot_tn(left, right):
    return contract(left, right, 0, 0)


def axis_count(axes):
    return math.prod(lax.axis_size(axis) for axis in axes)


def shape_of(*dims):
    return jax.ShapeDtypeStruct(dims, jnp.float32)


def call(body, outs, operands, far=(), scalars=0, flops=0, limit=VMEM_BYTES):
    specs = [SCALAR] * scalars + [WHOLE] * (len(operands) - scalars)
    specs += [pl.BlockSpec(memory_space=pltpu.HBM)] * len(far)
    operands = [*operands, *far]
    moved = sum(4 * operand.size for operand in operands) + sum(
        4 * math.prod(out.shape) for out in outs
    )
    scratch = [pltpu.VMEM(operand.shape, operand.dtype) for operand in far]
    if far:
        scratch.append(pltpu.SemaphoreType.DMA((len(far),)))
    return pl.pallas_call(
        body,
        out_shape=outs,
        in_specs=specs,
        out_specs=[WHOLE] * len(outs),
        scratch_shapes=scratch,
        compiler_params=pltpu.CompilerParams(vmem_limit_bytes=limit),
        cost_estimate=pl.CostEstimate(flops=flops, bytes_accessed=moved, transcendentals=0),
    )(*operands)


def fetch(far, copies, semaphores):
    moves = [
        pltpu.make_async_copy(source, target, semaphores.at[at])
        for at, (source, target) in enumerate(zip(far, copies))
    ]
    for move in moves:
        move.start()

    def read(at):
        moves[at].wait()
        return copies[at][...]

    return read


def iota(shape, dim):
    return lax.broadcasted_iota(jnp.int32, shape, dim)


def halves_up(wide):
    count = wide.shape[1] // LANES
    return jnp.concatenate(
        [wide[:, LANES * at : LANES * (at + 1)] for at in range(count)], axis=0
    )


def halves_down(tall, rows):
    count = tall.shape[0] // rows
    return jnp.concatenate([tall[rows * at : rows * (at + 1)] for at in range(count)], axis=1)


def exchange(blocks, axes):
    return lax.all_to_all(blocks, axes, 0, 0, tiled=True)


def gather_blocks(block, axes):
    count = axis_count(axes)
    return exchange(jnp.broadcast_to(block[None], (count,) + block.shape), axes)


def spread_kernel(scale, in_ref, out_ref):
    total = jnp.sum(in_ref[...], axis=0) * scale
    out_ref[...] = jnp.broadcast_to(total[None], out_ref.shape)


def sum_over(tall, axes, scale=1.0):
    count = axis_count(axes)
    size = tall.size
    depth = -(-size // (count * LANES))
    blocks = tall
    if size != count * depth * LANES:
        blocks = jnp.pad(tall.reshape(-1), (0, count * depth * LANES - size))
    blocks = blocks.reshape(count, depth, LANES)
    received = exchange(blocks, axes)
    (spread,) = call(
        functools.partial(spread_kernel, scale), [shape_of(count, depth, LANES)], [received]
    )
    whole = exchange(spread, axes)
    if size != count * depth * LANES:
        whole = whole.reshape(-1)[:size]
    return whole.reshape(tall.shape)


def is_power_of_two(count):
    return count & (count - 1) == 0


def hop(value, axes, low, width):
    count = axis_count(axes)
    total = value
    for pattern in range(1, 1 << width):
        pairs = [(source, source ^ (pattern << low)) for source in range(count)]
        total = total + lax.ppermute(value, axes, pairs)
    return total


def halves_of(tall, axes):
    half = tall.shape[0] // 2
    odd = lax.axis_index(axes) % 2 == 1
    kept = jnp.where(odd, tall[half:], tall[:half])
    return kept, jnp.where(odd, tall[:half], tall[half:])


def swap_pair(value, axes):
    count = axis_count(axes)
    return lax.ppermute(value, axes, [(source, source ^ 1) for source in range(count)])


def join_halves(mine, other, axes):
    odd = lax.axis_index(axes) % 2 == 1
    return jnp.concatenate([jnp.where(odd, other, mine), jnp.where(odd, mine, other)])


def half_by_hops(kept, sent, axes, upward):
    total = kept + swap_pair(sent, axes)
    spans = spans_of(axis_count(axes).bit_length() - 1)
    if upward:
        spans.reverse()
    for low, width in spans:
        total = hop(total, axes, low, width)
    return total


def sum_by_hops(kept, sent, axes, scale, upward):
    total = half_by_hops(kept, sent, axes, upward) * scale
    return join_halves(total, swap_pair(total, axes), axes)


def by_hops(count):
    return is_power_of_two(count) and 1 < count <= HOP_DEVICES


def sum_all(tall, axes, scale, upward):
    if by_hops(axis_count(axes)) and tall.shape[0] % (2 * SUBLANES) == 0:
        return sum_by_hops(*halves_of(tall, axes), axes, scale, upward)
    return sum_over(tall, axes, scale)


def swap_by_bits(blocks, position):
    size, bit = len(blocks), 0
    while 1 << bit < size:
        flip = ((position >> bit) & 1) == 1
        blocks = [
            jnp.where(flip, blocks[slot ^ (1 << bit)], blocks[slot]) for slot in range(size)
        ]
        bit += 1
    return blocks


def spans_of(bits):
    spans, low = [], bits
    while low > 1:
        width = min(HOP_BITS, low - 1)
        low -= width
        spans.append((low, width))
    return spans


def gather_rows(rows, axes):
    count = axis_count(axes)
    here = lax.axis_index(axes)
    held = rows
    places, size = [0], 1
    spans = spans_of(count.bit_length() - 1)
    for low, width in spans:
        blocks = [held]
        for pattern in range(1, 1 << width):
            pairs = [(source, source ^ (pattern << low)) for source in range(count)]
            blocks.append(lax.ppermute(held, axes, pairs))
        held = jnp.concatenate(swap_by_bits(blocks, here >> low))
        places = [digit * size + place for place in places for digit in range(1 << width)]
        size <<= width
    return held, swap_pair(held, axes), places


def leaf_kernel(count, at_ref, *refs):
    far, (y_ref, kept_ref, sent_ref, *packed_ref) = refs[:count], refs[count : -count - 1]
    read = fetch(far, refs[-count - 1 : -1], refs[-1])
    b_leaf, linv = read(0), read(1)
    y_leaf = dot_nt(b_leaf, linv)
    y_ref[...] = y_leaf
    contrib = dot_nt(y_leaf, read(2))
    rows = read(3)
    b_sep = read(4)
    extent = rows.shape[1]
    width = 2 * kept_ref.shape[0] // b_leaf.shape[0] * LANES
    hits = iota((width, extent), 0) == rows
    placed = dot_nt(contrib, hits.astype(jnp.float32))
    own_rows = b_sep.shape[0]
    own = iota((own_rows, width), 1) == iota((own_rows, width), 0) + at_ref[0]
    tall = halves_up(dot_tn(b_sep, own.astype(jnp.float32)) - placed)
    half = kept_ref.shape[0]
    odd = (at_ref[0] // own_rows) % 2 == 1
    kept_ref[...] = jnp.where(odd, tall[half:], tall[:half])
    sent_ref[...] = jnp.where(odd, tall[:half], tall[half:])
    if packed_ref:
        pack_rows(at_ref[0], [read(at) for at in range(5, count)], packed_ref[0])


def pack_rows(at, values, out_ref):
    sep_l, sep_u, lower, upper, root_l, root_u, b_root = values
    rows, width = sep_l.shape
    own = iota((rows, width), 0) + at
    col = iota((rows, width), 1)

    def fold(lower, upper):
        diagonal = jnp.sum(jnp.where(col == own, lower, 0.0), axis=1, keepdims=True)
        return jnp.where(col < own, lower, upper), diagonal

    sep, sep_diagonal = fold(sep_l, sep_u)
    root, root_diagonal = fold(root_l, root_u)
    quarter = (LANES - b_root.shape[1]) // 2
    extra = jnp.concatenate(
        [
            b_root,
            jnp.broadcast_to(sep_diagonal, (rows, quarter)),
            jnp.broadcast_to(root_diagonal, (rows, quarter)),
        ],
        axis=1,
    )
    out_ref[...] = halves_up(jnp.concatenate([sep, lower, upper, root, extra], axis=1))


def fold_kernel(
    at_ref, y_ref, rows_ref, upper_ref, uinv_ref, q_ref, q_sep_ref, y_out_ref, carry_ref
):
    extent = y_ref.shape[1]
    width = carry_ref.shape[0]
    hits = (iota((width, extent), 0) == rows_ref[...]).astype(jnp.float32)
    carried = dot_nt(hits, upper_ref[...])
    both = jnp.concatenate([y_ref[...], carried], axis=0)
    solved = dot_nt(both, uinv_ref[...])
    projected = dot_nn(solved, q_ref[...])
    ports = y_ref.shape[0]
    y_out_ref[:, :extent] = solved[:ports]
    y_out_ref[:, extent:] = projected[:ports]
    carry_ref[:, :extent] = solved[ports:]
    carry_ref[:, extent:] = projected[ports:]
    own = pl.ds(pl.multiple_of(at_ref[0], SUBLANES), q_sep_ref.shape[0])
    carry_ref[own, extent:] = carry_ref[own, extent:] - q_sep_ref[...]


def solve_kernel(
    places,
    at_ref,
    half_ref,
    pair_ref,
    mine_ref,
    other_ref,
    y_ref,
    carry_ref,
    q_root_ref,
    x_ref,
    partial_ref,
):
    ports = y_ref.shape[0]
    own_rows = SUBLANES
    width = 2 * len(places) * own_rows
    tall = mine_ref.shape[0] // len(places)
    odd = (at_ref[0] // own_rows) % 2 == 1

    def ordered(mine, other):
        return jnp.where(odd, other, mine), jnp.where(odd, mine, other)

    def piece(first, size):
        strips = []
        for lane in range(first // LANES, (first + size) // LANES):
            blocks = []
            for place in places:
                start = place * tall + lane * own_rows
                rows = slice(start, start + own_rows)
                blocks.extend(ordered(mine_ref[rows], other_ref[rows]))
            strips.append(jnp.concatenate(blocks, axis=0))
        return jnp.concatenate(strips, axis=1)

    row = iota((width, width), 0)
    col = iota((width, width), 1)

    def unfold(folded, diagonal):
        lower = jnp.where(col < row, folded, jnp.where(col == row, diagonal, 0.0))
        return lower, jnp.where(col >= row, folded, 0.0)

    extra = piece(4 * width, LANES)
    quarter = (LANES - ports) // 2
    sep_l, sep_u = unfold(piece(0, width), extra[:, ports : ports + 1])
    root_l, root_u = unfold(
        piece(3 * width, width), extra[:, ports + quarter : ports + quarter + 1]
    )
    b_root = extra.T[:ports]
    sources = halves_down(jnp.concatenate(ordered(half_ref[...], pair_ref[...]), axis=0), ports)
    y_sep = dot_nt(sources, sep_l)
    y_root = dot_nt(b_root - dot_nn(y_sep, piece(width, width)), root_l)
    x_root = dot_nt(y_root, root_u)
    x_sep = dot_nt(y_sep - dot_nt(x_root, piece(2 * width, width)), sep_u)
    own = iota((LANES, width), 1) - at_ref[0] == iota((LANES, width), 0)
    own = (own & (iota((LANES, width), 0) < own_rows)).astype(jnp.float32)
    root_own = dot_nt(x_root, own)[:, :own_rows]
    folded = y_ref[...] - dot_nn(x_sep, carry_ref[...])
    extent = y_ref.shape[1] - q_root_ref.shape[1]
    partial_ref[...] = halves_up(folded[:, extent:] + dot_nn(root_own, q_root_ref[...]))
    x_ref[:, :extent] = folded[:, :extent]
    sep_own = dot_nt(x_sep, own)[:, :own_rows]
    pad = jnp.zeros((ports, LANES - 2 * own_rows), jnp.float32)
    x_ref[:, extent:] = jnp.concatenate([sep_own, root_own, pad], axis=1)


def dense_kernel(cols_ref, g_ref, c_ref, g_out_ref, c_out_ref):
    block_rows, stored = cols_ref.shape
    size = g_ref.shape[1]
    for blocks_ref, out_ref in ((g_ref, g_out_ref), (c_ref, c_out_ref)):
        for row in range(block_rows):
            for col in range(block_rows):
                total = jnp.zeros((size, size), jnp.float32)
                for slot in range(stored):
                    start = (row * stored + slot) * size
                    block = blocks_ref[start : start + size, :]
                    total = total + jnp.where(cols_ref[row, slot] == col, block, 0.0)
                out_ref[size * row : size * (row + 1), size * col : size * (col + 1)] = total


def clean_kernel(
    coef_ref, x_ref, q_leaf_ref, q_sep_ref, q_root_ref, g_ref, c_ref, coef_out, clean_out, out_ref
):
    ports, extent = x_ref.shape[0], q_leaf_ref.shape[0]
    coef = halves_down(coef_ref[...], ports)
    coef_out[...] = coef
    leaf = x_ref[:, :extent] - dot_nt(coef, q_leaf_ref[...])
    q_own = jnp.concatenate([q_sep_ref[...], q_root_ref[...]], axis=0)
    pad = LANES - q_own.shape[0]
    q_own = jnp.concatenate([q_own, jnp.zeros((pad, q_own.shape[1]), jnp.float32)], axis=0)
    own = x_ref[:, extent:] - dot_nt(coef, q_own)
    clean_out[:, :extent] = leaf
    clean_out[:, extent:] = own
    images = dot_nt(leaf, jnp.concatenate([g_ref[...], c_ref[...]], axis=0))
    products = dot_nt(
        leaf, jnp.concatenate([leaf, images[:, :extent], images[:, extent:]], axis=0)
    )
    gram = products[:, :ports] + dot_nt(own, own)
    out_ref[:ports, :] = jnp.concatenate([gram, products[:, ports : 2 * ports]], axis=1)
    out_ref[ports:, :] = jnp.concatenate([gram, products[:, 2 * ports :]], axis=1)


def eliminate(tiles, offset, step):
    shape = tiles[0].shape
    rows = iota(shape, 0)
    tiles = list(tiles)

    def whole_row(tile, at):
        return jnp.broadcast_to(tile[at : at + 1, :], shape)

    def whole_col(tile, at):
        return jnp.broadcast_to(tile[:, at : at + 1], shape)

    for first in range(0, len(tiles) * SUBLANES, step):
        top, base = divmod(first, SUBLANES)
        pivots = [whole_row(tiles[top], base + t) for t in range(step)]
        columns = [
            [whole_col(tile, offset + first + t) for tile in tiles[top:]] for t in range(step)
        ]
        corner = [[whole_row(columns[u][0], base + t) for u in range(step)] for t in range(step)]
        factors = []
        for t in range(step):
            inverse = 1.0 / corner[t][t]
            for u in range(t + 1, step):
                ratio = corner[u][t] * inverse
                pivots[u] = pivots[u] - ratio * pivots[t]
                for v in range(t + 1, step):
                    corner[u][v] = corner[u][v] - ratio * corner[t][v]
            factor = [column * inverse for column in columns[t]]
            for v in range(t + 1, step):
                columns[v] = [c - f * corner[t][v] for c, f in zip(columns[v], factor)]
            factor[0] = jnp.where(rows > base + t, factor[0], 0.0)
            factors.append(factor)
        for at in range(top, len(tiles)):
            value = tiles[at]
            for t in range(step):
                value = value - factors[t][at - top] * pivots[t]
            tiles[at] = value
    return tiles


def factor_kernel(half_ref, inverse_ref):
    ports = inverse_ref.shape[0]
    diagonal = iota((ports, ports), 0) == iota((ports, ports), 1)
    joined = jnp.concatenate([jnp.where(diagonal, 1.0, 0.0), half_ref[:, :ports]], axis=1)
    tiles = [joined[at : at + SUBLANES] for at in range(0, ports, SUBLANES)]
    joined = jnp.concatenate(eliminate(tiles, ports, SUBLANES), axis=0)
    pivots = jnp.sum(jnp.where(diagonal, joined[:, ports:], 0.0), axis=1, keepdims=True)
    inverse = joined[:, :ports] / jnp.sqrt(pivots)
    inverse_ref[...] = inverse


def finish_kernel(
    at_ref, half_ref, pair_ref, inverse_ref, clean_ref, v_leaf_ref, v_sep_ref, v_root_ref, g_ref, c_ref
):
    ports = inverse_ref.shape[0]
    extent = v_leaf_ref.shape[1]
    own_rows = v_sep_ref.shape[0]
    inverse = inverse_ref[...]
    left = dot_nn(
        inverse,
        jnp.concatenate([half_ref[:, ports:], pair_ref[:, ports:], clean_ref[...]], axis=1),
    )
    v_leaf_ref[...] = left[:, LANES : LANES + extent]
    own = left[:, LANES + extent :].T
    v_sep_ref[...] = own[:own_rows]
    v_root_ref[...] = own[own_rows : 2 * own_rows]
    left = jnp.concatenate([left[:, :ports], left[:, ports : 2 * ports]], axis=0)
    whole = dot_nt(left, inverse)
    odd = at_ref[0] == 1
    g_ref[...] = jnp.where(odd, whole[ports:], whole[:ports])
    c_ref[...] = jnp.where(odd, whole[:ports], whole[ports:])


def solve_replicated(at, kept, sent, packed, y_leaf, late):
    ports, extent = y_leaf.shape
    basis = late[-1].shape[1]
    rows, upper, uinv, q_leaf, q_sep, q_root = late
    width = 2 * kept.shape[0] // ports * LANES
    folded, carry = call(
        fold_kernel,
        [shape_of(ports, extent + basis), shape_of(width, extent + basis)],
        [at, y_leaf, rows, upper, uinv, q_leaf, q_sep],
        scalars=1,
        flops=30 * extent * extent * ports,
    )
    mine, other, places = gather_rows(packed, GROUP)
    half = half_by_hops(kept, sent, GROUP, FIRST_UPWARD)
    pair = swap_pair(half, GROUP)
    return call(
        functools.partial(solve_kernel, places),
        [shape_of(ports, extent + LANES), shape_of(basis // LANES * ports, LANES)],
        [at, half, pair, mine, other, folded, carry, q_root],
        scalars=1,
        flops=22 * extent * extent * ports,
    )


def solve_spread(at, sources, b_root, factors, leaf, bases):
    sep_linv, sep_uinv, sep_lower, sep_upper, root_linv, root_uinv = factors
    y_leaf, sep_rows, leaf_upper, leaf_uinv = leaf
    ports = y_leaf.shape[0]
    sep_local, sep_width = sep_linv.shape
    root_local, root_width = root_linv.shape
    row = iota((sep_local, sep_width), 0) + at[0]
    col = iota((sep_local, sep_width), 1)
    diagonal = jnp.sum(jnp.where(row == col, sep_linv, 0.0), axis=1, keepdims=True)
    folded = jnp.concatenate(
        [jnp.where(col < row, sep_linv, sep_uinv), jnp.broadcast_to(diagonal, (sep_local, LANES))],
        axis=1,
    )
    pair = gather_blocks(folded, GROUP).reshape(sep_width, -1)
    row = iota((sep_width, sep_width), 0)
    col = iota((sep_width, sep_width), 1)
    square = pair[:, :sep_width]
    sep_l = jnp.where(col < row, square, jnp.where(col == row, pair[:, sep_width:][:, :1], 0.0))
    sep_u = jnp.where(col >= row, square, 0.0)

    def own_rows(value):
        return lax.dynamic_slice(value, (at[0], 0), (sep_local, ports))

    y_sep = contract(sep_l, halves_down(sources, ports), 1, 1)
    count = axis_count(EVERYONE)
    update = contract(sep_lower, own_rows(y_sep), 1, 0).reshape(count, root_local, ports)
    held = b_root - exchange(update, EVERYONE).sum(axis=0)
    for factor in (root_linv, root_uinv):
        whole = gather_blocks(held, EVERYONE).reshape(root_width, ports)
        held = contract(factor, whole, 1, 0)
    x_root = held
    whole = gather_blocks(x_root, EVERYONE).reshape(root_width, ports)
    z_sep = own_rows(y_sep) - contract(sep_upper, whole, 1, 0)
    whole = gather_blocks(z_sep, GROUP).reshape(sep_width, ports)
    x_sep = contract(sep_u, whole, 1, 0)
    coupled = x_sep[sep_rows[0]]
    inner = y_leaf - contract(coupled, leaf_upper, 0, 1)
    x_leaf = contract(inner, leaf_uinv, 1, 1)
    own = jnp.concatenate([own_rows(x_sep), x_root], axis=0)
    partial = contract(x_leaf, bases[0], 1, 0) + contract(
        own, jnp.concatenate(bases[1:], axis=0), 0, 0
    )
    pad = jnp.zeros((ports, LANES - own.shape[0]), jnp.float32)
    return jnp.concatenate([x_leaf, own.T, pad], axis=1), halves_up(partial)


def shards(
    b_leaf,
    b_sep,
    b_root,
    leaf_linv,
    leaf_uinv,
    leaf_lower,
    leaf_upper,
    sep_rows,
    sep_linv,
    sep_uinv,
    sep_lower,
    sep_upper,
    root_linv,
    root_uinv,
    basis_leaf,
    basis_sep,
    basis_root,
    g_blocks,
    c_blocks,
    block_cols,
):
    extent, ports = b_leaf.shape
    sep_local = b_sep.shape[0]
    root_local = b_root.shape[0]
    sep_width = sep_linv.shape[1]
    basis = basis_leaf.shape[1]
    at = (lax.axis_index(GROUP) * sep_local).astype(jnp.int32).reshape(1)
    count = axis_count(EVERYONE)
    node_count = float(count * (extent + sep_local + root_local))
    square = extent * extent * ports

    factors = (sep_linv, sep_uinv, sep_lower, sep_upper, root_linv, root_uinv)
    bases = (basis_leaf, basis_sep, basis_root)
    replicate = (
        count == axis_count(GROUP)
        and sep_local == root_local == SUBLANES
        and by_hops(count)
        and 4 * sep_width * (4 * sep_width + LANES) <= REPLICATE_BYTES
    )
    tall = sep_width // LANES * ports
    outs = [shape_of(ports, extent), shape_of(tall // 2, LANES), shape_of(tall // 2, LANES)]
    far = [b_leaf.T, leaf_linv, leaf_lower, sep_rows, b_sep]
    if replicate:
        outs.append(shape_of((4 * sep_width // LANES + 1) * sep_local, LANES))
        far += [sep_linv, sep_uinv, sep_lower.T, sep_upper, root_linv, root_uinv, b_root]
    y_leaf, kept, sent, *packed = call(
        functools.partial(leaf_kernel, len(far)),
        outs,
        [at],
        far=far,
        scalars=1,
        flops=6 * square,
        limit=None,
    )
    if replicate:
        late = [sep_rows, leaf_upper, leaf_uinv, *bases]
        x_all, partial = solve_replicated(at, kept, sent, *packed, y_leaf, late)
    else:
        if by_hops(axis_count(GROUP)):
            sources = sum_by_hops(kept, sent, GROUP, 1.0, False)
        else:
            sources = sum_over(join_halves(kept, sent, GROUP), GROUP)
        leaf = (y_leaf, sep_rows, leaf_upper, leaf_uinv)
        x_all, partial = solve_spread(at, sources, b_root, factors, leaf, bases)
    coefficients = sum_all(partial, EVERYONE, 1.0 / node_count, True)
    g_dense, c_dense = call(
        dense_kernel, [shape_of(extent, extent)] * 2, [block_cols, g_blocks, c_blocks], scalars=1
    )
    coef_out, cleaned, products = call(
        clean_kernel,
        [shape_of(ports, basis), shape_of(ports, extent + LANES), shape_of(2 * ports, LANES)],
        [coefficients, x_all, basis_leaf, basis_sep, basis_root, g_dense, c_dense],
        flops=14 * square,
    )
    parity = (lax.axis_index(EVERYONE) % 2).astype(jnp.int32).reshape(1)
    if by_hops(count):
        kept, sent = halves_of(products, EVERYONE)
        half = half_by_hops(kept, sent, EVERYONE, False) * (1.0 / node_count)
        pair = swap_pair(half, EVERYONE)
    else:
        sums = sum_over(products, EVERYONE, 1.0 / node_count)
        half, pair = halves_of(sums, EVERYONE)
    (inverse,) = call(factor_kernel, [shape_of(ports, ports)], [half])
    v_leaf, v_sep, v_root, g_out, c_out = call(
        finish_kernel,
        [
            shape_of(ports, extent),
            shape_of(sep_local, ports),
            shape_of(root_local, ports),
            shape_of(ports, ports),
            shape_of(ports, ports),
        ],
        [parity, half, pair, inverse, cleaned],
        scalars=1,
        flops=4 * square,
    )
    return (v_leaf.T, v_sep, v_root, coef_out.T, g_out, c_out)


def solution(mesh):
    rows = P(EVERYONE, None)
    columns = P(None, EVERYONE)
    return jax.shard_map(
        shards,
        mesh=mesh,
        in_specs=(rows,) * 10 + (columns,) + (rows,) * 9,
        out_specs=(rows, rows, rows, P(), P(), P()),
        check_vma=False,
    )
```

```python
import functools
import math

import jax
import jax.numpy as jnp
from jax import lax
from jax.experimental import pallas as pl
from jax.experimental.pallas import tpu as pltpu
from jax.sharding import PartitionSpec as P


LANES = 128
SUBLANES = 8
REPLICATE_BYTES = 4 << 20
VMEM_BYTES = 12 << 20
HOP_BITS = 2
HOP_DEVICES = 64
FIRST_UPWARD = True
EVERYONE = ("outer", "inner")
GROUP = ("inner",)
WHOLE = pl.BlockSpec(memory_space=pltpu.VMEM)
SCALAR = pl.BlockSpec(memory_space=pltpu.SMEM)


def contract(left, right, left_dim, right_dim, precision=lax.Precision.HIGHEST):
    return lax.dot_general(
        left,
        right,
        (((left_dim,), (right_dim,)), ((), ())),
        precision=precision,
        preferred_element_type=jnp.float32,
    )


def parts_of(value):
    high = value.astype(jnp.bfloat16)
    return high, (value - high.astype(jnp.float32)).astype(jnp.bfloat16)


def dot_parts(left, right, right_dim):
    rows = left.shape[0]
    high, middle = parts_of(left)
    first, second = parts_of(right)
    two = contract(jnp.concatenate([high, middle], axis=0), first, 1, right_dim, None)
    one = contract(high, second, 1, right_dim, None)
    return two[:rows] + (two[rows:] + one)


def dot_nn(left, right):
    return dot_parts(left, right, 0)


def dot_nt(left, right):
    return dot_parts(left, right, 1)


def dot_tn(left, right):
    return contract(left, right, 0, 0)


def axis_count(axes):
    return math.prod(lax.axis_size(axis) for axis in axes)


def shape_of(*dims):
    return jax.ShapeDtypeStruct(dims, jnp.float32)


def call(body, outs, operands, far=(), scalars=0, flops=0, limit=VMEM_BYTES):
    specs = [SCALAR] * scalars + [WHOLE] * (len(operands) - scalars)
    specs += [pl.BlockSpec(memory_space=pltpu.HBM)] * len(far)
    operands = [*operands, *far]
    moved = sum(4 * operand.size for operand in operands) + sum(
        4 * math.prod(out.shape) for out in outs
    )
    scratch = [pltpu.VMEM(operand.shape, operand.dtype) for operand in far]
    if far:
        scratch.append(pltpu.SemaphoreType.DMA((len(far),)))
    return pl.pallas_call(
        body,
        out_shape=outs,
        in_specs=specs,
        out_specs=[WHOLE] * len(outs),
        scratch_shapes=scratch,
        compiler_params=pltpu.CompilerParams(vmem_limit_bytes=limit),
        cost_estimate=pl.CostEstimate(flops=flops, bytes_accessed=moved, transcendentals=0),
    )(*operands)


def fetch(far, copies, semaphores):
    moves = [
        pltpu.make_async_copy(source, target, semaphores.at[at])
        for at, (source, target) in enumerate(zip(far, copies))
    ]
    for move in moves:
        move.start()

    def read(at):
        moves[at].wait()
        return copies[at][...]

    return read


def iota(shape, dim):
    return lax.broadcasted_iota(jnp.int32, shape, dim)


def halves_up(wide):
    count = wide.shape[1] // LANES
    return jnp.concatenate(
        [wide[:, LANES * at : LANES * (at + 1)] for at in range(count)], axis=0
    )


def halves_down(tall, rows):
    count = tall.shape[0] // rows
    return jnp.concatenate([tall[rows * at : rows * (at + 1)] for at in range(count)], axis=1)


def exchange(blocks, axes):
    return lax.all_to_all(blocks, axes, 0, 0, tiled=True)


def gather_blocks(block, axes):
    count = axis_count(axes)
    return exchange(jnp.broadcast_to(block[None], (count,) + block.shape), axes)


def spread_kernel(scale, in_ref, out_ref):
    total = jnp.sum(in_ref[...], axis=0) * scale
    out_ref[...] = jnp.broadcast_to(total[None], out_ref.shape)


def sum_over(tall, axes, scale=1.0):
    count = axis_count(axes)
    size = tall.size
    depth = -(-size // (count * LANES))
    blocks = tall
    if size != count * depth * LANES:
        blocks = jnp.pad(tall.reshape(-1), (0, count * depth * LANES - size))
    blocks = blocks.reshape(count, depth, LANES)
    received = exchange(blocks, axes)
    (spread,) = call(
        functools.partial(spread_kernel, scale), [shape_of(count, depth, LANES)], [received]
    )
    whole = exchange(spread, axes)
    if size != count * depth * LANES:
        whole = whole.reshape(-1)[:size]
    return whole.reshape(tall.shape)


def is_power_of_two(count):
    return count & (count - 1) == 0


def hop(value, axes, low, width):
    count = axis_count(axes)
    total = value
    for pattern in range(1, 1 << width):
        pairs = [(source, source ^ (pattern << low)) for source in range(count)]
        total = total + lax.ppermute(value, axes, pairs)
    return total


def halves_of(tall, axes):
    half = tall.shape[0] // 2
    odd = lax.axis_index(axes) % 2 == 1
    kept = jnp.where(odd, tall[half:], tall[:half])
    return kept, jnp.where(odd, tall[:half], tall[half:])


def swap_pair(value, axes):
    count = axis_count(axes)
    return lax.ppermute(value, axes, [(source, source ^ 1) for source in range(count)])


def join_halves(mine, other, axes):
    odd = lax.axis_index(axes) % 2 == 1
    return jnp.concatenate([jnp.where(odd, other, mine), jnp.where(odd, mine, other)])


def half_by_hops(kept, sent, axes, upward):
    total = kept + swap_pair(sent, axes)
    spans = spans_of(axis_count(axes).bit_length() - 1)
    if upward:
        spans.reverse()
    for low, width in spans:
        total = hop(total, axes, low, width)
    return total


def sum_by_hops(kept, sent, axes, scale, upward):
    total = half_by_hops(kept, sent, axes, upward) * scale
    return join_halves(total, swap_pair(total, axes), axes)


def by_hops(count):
    return is_power_of_two(count) and 1 < count <= HOP_DEVICES


def sum_all(tall, axes, scale, upward):
    if by_hops(axis_count(axes)) and tall.shape[0] % (2 * SUBLANES) == 0:
        return sum_by_hops(*halves_of(tall, axes), axes, scale, upward)
    return sum_over(tall, axes, scale)


def swap_by_bits(blocks, position):
    size, bit = len(blocks), 0
    while 1 << bit < size:
        flip = ((position >> bit) & 1) == 1
        blocks = [
            jnp.where(flip, blocks[slot ^ (1 << bit)], blocks[slot]) for slot in range(size)
        ]
        bit += 1
    return blocks


def spans_of(bits):
    spans, low = [], bits
    while low > 1:
        width = min(HOP_BITS, low - 1)
        low -= width
        spans.append((low, width))
    return spans


def gather_rows(rows, axes):
    count = axis_count(axes)
    here = lax.axis_index(axes)
    held = rows
    places, size = [0], 1
    spans = spans_of(count.bit_length() - 1)
    for low, width in spans:
        blocks = [held]
        for pattern in range(1, 1 << width):
            pairs = [(source, source ^ (pattern << low)) for source in range(count)]
            blocks.append(lax.ppermute(held, axes, pairs))
        held = jnp.concatenate(swap_by_bits(blocks, here >> low))
        places = [digit * size + place for place in places for digit in range(1 << width)]
        size <<= width
    return held, swap_pair(held, axes), places


def leaf_kernel(count, at_ref, *refs):
    far, (y_ref, kept_ref, sent_ref, *packed_ref) = refs[:count], refs[count : -count - 1]
    read = fetch(far, refs[-count - 1 : -1], refs[-1])
    b_leaf, linv = read(0), read(1)
    y_leaf = dot_nt(b_leaf, linv)
    y_ref[...] = y_leaf
    contrib = dot_nt(y_leaf, read(2))
    rows = read(3)
    b_sep = read(4)
    extent = rows.shape[1]
    width = 2 * kept_ref.shape[0] // b_leaf.shape[0] * LANES
    hits = iota((width, extent), 0) == rows
    placed = dot_nt(contrib, hits.astype(jnp.float32))
    own_rows = b_sep.shape[0]
    own = iota((own_rows, width), 1) == iota((own_rows, width), 0) + at_ref[0]
    tall = halves_up(dot_tn(b_sep, own.astype(jnp.float32)) - placed)
    half = kept_ref.shape[0]
    odd = (at_ref[0] // own_rows) % 2 == 1
    kept_ref[...] = jnp.where(odd, tall[half:], tall[:half])
    sent_ref[...] = jnp.where(odd, tall[:half], tall[half:])
    if packed_ref:
        pack_rows(at_ref[0], [read(at) for at in range(5, count)], packed_ref[0])


def pack_rows(at, values, out_ref):
    sep_l, sep_u, lower, upper, root_l, root_u, b_root = values
    rows, width = sep_l.shape
    own = iota((rows, width), 0) + at
    col = iota((rows, width), 1)

    def fold(lower, upper):
        diagonal = jnp.sum(jnp.where(col == own, lower, 0.0), axis=1, keepdims=True)
        return jnp.where(col < own, lower, upper), diagonal

    sep, sep_diagonal = fold(sep_l, sep_u)
    root, root_diagonal = fold(root_l, root_u)
    quarter = (LANES - b_root.shape[1]) // 2
    extra = jnp.concatenate(
        [
            b_root,
            jnp.broadcast_to(sep_diagonal, (rows, quarter)),
            jnp.broadcast_to(root_diagonal, (rows, quarter)),
        ],
        axis=1,
    )
    out_ref[...] = halves_up(jnp.concatenate([sep, lower, upper, root, extra], axis=1))


def fold_kernel(
    at_ref, y_ref, rows_ref, upper_ref, uinv_ref, q_ref, q_sep_ref, y_out_ref, carry_ref
):
    extent = y_ref.shape[1]
    width = carry_ref.shape[0]
    hits = (iota((width, extent), 0) == rows_ref[...]).astype(jnp.float32)
    carried = dot_nt(hits, upper_ref[...])
    both = jnp.concatenate([y_ref[...], carried], axis=0)
    solved = dot_nt(both, uinv_ref[...])
    projected = dot_nn(solved, q_ref[...])
    ports = y_ref.shape[0]
    y_out_ref[:, :extent] = solved[:ports]
    y_out_ref[:, extent:] = projected[:ports]
    carry_ref[:, :extent] = solved[ports:]
    carry_ref[:, extent:] = projected[ports:]
    own = pl.ds(pl.multiple_of(at_ref[0], SUBLANES), q_sep_ref.shape[0])
    carry_ref[own, extent:] = carry_ref[own, extent:] - q_sep_ref[...]


def solve_kernel(
    places,
    at_ref,
    half_ref,
    pair_ref,
    mine_ref,
    other_ref,
    y_ref,
    carry_ref,
    q_root_ref,
    x_ref,
    partial_ref,
):
    ports = y_ref.shape[0]
    own_rows = SUBLANES
    width = 2 * len(places) * own_rows
    tall = mine_ref.shape[0] // len(places)
    odd = (at_ref[0] // own_rows) % 2 == 1

    def ordered(mine, other):
        return jnp.where(odd, other, mine), jnp.where(odd, mine, other)

    def piece(first, size):
        strips = []
        for lane in range(first // LANES, (first + size) // LANES):
            blocks = []
            for place in places:
                start = place * tall + lane * own_rows
                rows = slice(start, start + own_rows)
                blocks.extend(ordered(mine_ref[rows], other_ref[rows]))
            strips.append(jnp.concatenate(blocks, axis=0))
        return jnp.concatenate(strips, axis=1)

    row = iota((width, width), 0)
    col = iota((width, width), 1)

    def unfold(folded, diagonal):
        lower = jnp.where(col < row, folded, jnp.where(col == row, diagonal, 0.0))
        return lower, jnp.where(col >= row, folded, 0.0)

    extra = piece(4 * width, LANES)
    quarter = (LANES - ports) // 2
    sep_l, sep_u = unfold(piece(0, width), extra[:, ports : ports + 1])
    root_l, root_u = unfold(
        piece(3 * width, width), extra[:, ports + quarter : ports + quarter + 1]
    )
    b_root = extra.T[:ports]
    sources = halves_down(jnp.concatenate(ordered(half_ref[...], pair_ref[...]), axis=0), ports)
    y_sep = dot_nt(sources, sep_l)
    y_root = dot_nt(b_root - dot_nn(y_sep, piece(width, width)), root_l)
    x_root = dot_nt(y_root, root_u)
    x_sep = dot_nt(y_sep - dot_nt(x_root, piece(2 * width, width)), sep_u)
    own = iota((LANES, width), 1) - at_ref[0] == iota((LANES, width), 0)
    own = (own & (iota((LANES, width), 0) < own_rows)).astype(jnp.float32)
    root_own = dot_nt(x_root, own)[:, :own_rows]
    folded = y_ref[...] - dot_nn(x_sep, carry_ref[...])
    extent = y_ref.shape[1] - q_root_ref.shape[1]
    partial_ref[...] = halves_up(folded[:, extent:] + dot_nn(root_own, q_root_ref[...]))
    x_ref[:, :extent] = folded[:, :extent]
    sep_own = dot_nt(x_sep, own)[:, :own_rows]
    pad = jnp.zeros((ports, LANES - 2 * own_rows), jnp.float32)
    x_ref[:, extent:] = jnp.concatenate([sep_own, root_own, pad], axis=1)


def dense_kernel(cols_ref, g_ref, c_ref, g_out_ref, c_out_ref):
    block_rows, stored = cols_ref.shape
    size = g_ref.shape[1]
    for blocks_ref, out_ref in ((g_ref, g_out_ref), (c_ref, c_out_ref)):
        for row in range(block_rows):
            for col in range(block_rows):
                total = jnp.zeros((size, size), jnp.float32)
                for slot in range(stored):
                    start = (row * stored + slot) * size
                    block = blocks_ref[start : start + size, :]
                    total = total + jnp.where(cols_ref[row, slot] == col, block, 0.0)
                out_ref[size * row : size * (row + 1), size * col : size * (col + 1)] = total


def clean_kernel(
    coef_ref, x_ref, q_leaf_ref, q_sep_ref, q_root_ref, g_ref, c_ref, coef_out, clean_out, out_ref
):
    ports, extent = x_ref.shape[0], q_leaf_ref.shape[0]
    coef = halves_down(coef_ref[...], ports)
    coef_out[...] = coef
    leaf = x_ref[:, :extent] - dot_nt(coef, q_leaf_ref[...])
    q_own = jnp.concatenate([q_sep_ref[...], q_root_ref[...]], axis=0)
    pad = LANES - q_own.shape[0]
    q_own = jnp.concatenate([q_own, jnp.zeros((pad, q_own.shape[1]), jnp.float32)], axis=0)
    own = x_ref[:, extent:] - dot_nt(coef, q_own)
    clean_out[:, :extent] = leaf
    clean_out[:, extent:] = own
    images = dot_nt(leaf, jnp.concatenate([g_ref[...], c_ref[...]], axis=0))
    products = dot_nt(
        leaf, jnp.concatenate([leaf, images[:, :extent], images[:, extent:]], axis=0)
    )
    gram = products[:, :ports] + dot_nt(own, own)
    out_ref[:ports, :] = jnp.concatenate([gram, products[:, ports : 2 * ports]], axis=1)
    out_ref[ports:, :] = jnp.concatenate([gram, products[:, 2 * ports :]], axis=1)


def eliminate(tiles, offset, step):
    shape = tiles[0].shape
    rows = iota(shape, 0)
    tiles = list(tiles)

    def whole_row(tile, at):
        return jnp.broadcast_to(tile[at : at + 1, :], shape)

    def whole_col(tile, at):
        return jnp.broadcast_to(tile[:, at : at + 1], shape)

    for first in range(0, len(tiles) * SUBLANES, step):
        top, base = divmod(first, SUBLANES)
        pivots = [whole_row(tiles[top], base + t) for t in range(step)]
        columns = [
            [whole_col(tile, offset + first + t) for tile in tiles[top:]] for t in range(step)
        ]
        corner = [[whole_row(columns[u][0], base + t) for u in range(step)] for t in range(step)]
        factors = []
        for t in range(step):
            inverse = 1.0 / corner[t][t]
            for u in range(t + 1, step):
                ratio = corner[u][t] * inverse
                pivots[u] = pivots[u] - ratio * pivots[t]
                for v in range(t + 1, step):
                    corner[u][v] = corner[u][v] - ratio * corner[t][v]
            factor = [column * inverse for column in columns[t]]
            for v in range(t + 1, step):
                columns[v] = [c - f * corner[t][v] for c, f in zip(columns[v], factor)]
            factor[0] = jnp.where(rows > base + t, factor[0], 0.0)
            factors.append(factor)
        for at in range(top, len(tiles)):
            value = tiles[at]
            for t in range(step):
                value = value - factors[t][at - top] * pivots[t]
            tiles[at] = value
    return tiles


def factor_kernel(half_ref, inverse_ref):
    ports = inverse_ref.shape[0]
    diagonal = iota((ports, ports), 0) == iota((ports, ports), 1)
    joined = jnp.concatenate([jnp.where(diagonal, 1.0, 0.0), half_ref[:, :ports]], axis=1)
    tiles = [joined[at : at + SUBLANES] for at in range(0, ports, SUBLANES)]
    joined = jnp.concatenate(eliminate(tiles, ports, SUBLANES), axis=0)
    pivots = jnp.sum(jnp.where(diagonal, joined[:, ports:], 0.0), axis=1, keepdims=True)
    inverse = joined[:, :ports] / jnp.sqrt(pivots)
    inverse_ref[...] = inverse


def finish_kernel(
    at_ref, half_ref, pair_ref, inverse_ref, clean_ref, v_leaf_ref, v_sep_ref, v_root_ref, g_ref, c_ref
):
    ports = inverse_ref.shape[0]
    extent = v_leaf_ref.shape[1]
    own_rows = v_sep_ref.shape[0]
    inverse = inverse_ref[...]
    left = dot_nn(
        inverse,
        jnp.concatenate([half_ref[:, ports:], pair_ref[:, ports:], clean_ref[...]], axis=1),
    )
    v_leaf_ref[...] = left[:, LANES : LANES + extent]
    own = left[:, LANES + extent :].T
    v_sep_ref[...] = own[:own_rows]
    v_root_ref[...] = own[own_rows : 2 * own_rows]
    left = jnp.concatenate([left[:, :ports], left[:, ports : 2 * ports]], axis=0)
    whole = dot_nt(left, inverse)
    odd = at_ref[0] == 1
    g_ref[...] = jnp.where(odd, whole[ports:], whole[:ports])
    c_ref[...] = jnp.where(odd, whole[:ports], whole[ports:])


def solve_replicated(at, kept, sent, packed, y_leaf, late):
    ports, extent = y_leaf.shape
    basis = late[-1].shape[1]
    rows, upper, uinv, q_leaf, q_sep, q_root = late
    width = 2 * kept.shape[0] // ports * LANES
    folded, carry = call(
        fold_kernel,
        [shape_of(ports, extent + basis), shape_of(width, extent + basis)],
        [at, y_leaf, rows, upper, uinv, q_leaf, q_sep],
        scalars=1,
        flops=30 * extent * extent * ports,
    )
    mine, other, places = gather_rows(packed, GROUP)
    half = half_by_hops(kept, sent, GROUP, FIRST_UPWARD)
    pair = swap_pair(half, GROUP)
    return call(
        functools.partial(solve_kernel, places),
        [shape_of(ports, extent + LANES), shape_of(basis // LANES * ports, LANES)],
        [at, half, pair, mine, other, folded, carry, q_root],
        scalars=1,
        flops=22 * extent * extent * ports,
    )


def solve_spread(at, sources, b_root, factors, leaf, bases):
    sep_linv, sep_uinv, sep_lower, sep_upper, root_linv, root_uinv = factors
    y_leaf, sep_rows, leaf_upper, leaf_uinv = leaf
    ports = y_leaf.shape[0]
    sep_local, sep_width = sep_linv.shape
    root_local, root_width = root_linv.shape
    row = iota((sep_local, sep_width), 0) + at[0]
    col = iota((sep_local, sep_width), 1)
    diagonal = jnp.sum(jnp.where(row == col, sep_linv, 0.0), axis=1, keepdims=True)
    folded = jnp.concatenate(
        [jnp.where(col < row, sep_linv, sep_uinv), jnp.broadcast_to(diagonal, (sep_local, LANES))],
        axis=1,
    )
    pair = gather_blocks(folded, GROUP).reshape(sep_width, -1)
    row = iota((sep_width, sep_width), 0)
    col = iota((sep_width, sep_width), 1)
    square = pair[:, :sep_width]
    sep_l = jnp.where(col < row, square, jnp.where(col == row, pair[:, sep_width:][:, :1], 0.0))
    sep_u = jnp.where(col >= row, square, 0.0)

    def own_rows(value):
        return lax.dynamic_slice(value, (at[0], 0), (sep_local, ports))

    y_sep = contract(sep_l, halves_down(sources, ports), 1, 1)
    count = axis_count(EVERYONE)
    update = contract(sep_lower, own_rows(y_sep), 1, 0).reshape(count, root_local, ports)
    held = b_root - exchange(update, EVERYONE).sum(axis=0)
    for factor in (root_linv, root_uinv):
        whole = gather_blocks(held, EVERYONE).reshape(root_width, ports)
        held = contract(factor, whole, 1, 0)
    x_root = held
    whole = gather_blocks(x_root, EVERYONE).reshape(root_width, ports)
    z_sep = own_rows(y_sep) - contract(sep_upper, whole, 1, 0)
    whole = gather_blocks(z_sep, GROUP).reshape(sep_width, ports)
    x_sep = contract(sep_u, whole, 1, 0)
    coupled = x_sep[sep_rows[0]]
    inner = y_leaf - contract(coupled, leaf_upper, 0, 1)
    x_leaf = contract(inner, leaf_uinv, 1, 1)
    own = jnp.concatenate([own_rows(x_sep), x_root], axis=0)
    partial = contract(x_leaf, bases[0], 1, 0) + contract(
        own, jnp.concatenate(bases[1:], axis=0), 0, 0
    )
    pad = jnp.zeros((ports, LANES - own.shape[0]), jnp.float32)
    return jnp.concatenate([x_leaf, own.T, pad], axis=1), halves_up(partial)


def shards(
    b_leaf,
    b_sep,
    b_root,
    leaf_linv,
    leaf_uinv,
    leaf_lower,
    leaf_upper,
    sep_rows,
    sep_linv,
    sep_uinv,
    sep_lower,
    sep_upper,
    root_linv,
    root_uinv,
    basis_leaf,
    basis_sep,
    basis_root,
    g_blocks,
    c_blocks,
    block_cols,
):
    extent, ports = b_leaf.shape
    sep_local = b_sep.shape[0]
    root_local = b_root.shape[0]
    sep_width = sep_linv.shape[1]
    basis = basis_leaf.shape[1]
    at = (lax.axis_index(GROUP) * sep_local).astype(jnp.int32).reshape(1)
    count = axis_count(EVERYONE)
    node_count = float(count * (extent + sep_local + root_local))
    square = extent * extent * ports

    factors = (sep_linv, sep_uinv, sep_lower, sep_upper, root_linv, root_uinv)
    bases = (basis_leaf, basis_sep, basis_root)
    replicate = (
        count == axis_count(GROUP)
        and sep_local == root_local == SUBLANES
        and by_hops(count)
        and 4 * sep_width * (4 * sep_width + LANES) <= REPLICATE_BYTES
    )
    tall = sep_width // LANES * ports
    outs = [shape_of(ports, extent), shape_of(tall // 2, LANES), shape_of(tall // 2, LANES)]
    far = [b_leaf.T, leaf_linv, leaf_lower, sep_rows, b_sep]
    if replicate:
        outs.append(shape_of((4 * sep_width // LANES + 1) * sep_local, LANES))
        far += [sep_linv, sep_uinv, sep_lower.T, sep_upper, root_linv, root_uinv, b_root]
    y_leaf, kept, sent, *packed = call(
        functools.partial(leaf_kernel, len(far)),
        outs,
        [at],
        far=far,
        scalars=1,
        flops=6 * square,
        limit=None,
    )
    if replicate:
        late = [sep_rows, leaf_upper, leaf_uinv, *bases]
        x_all, partial = solve_replicated(at, kept, sent, *packed, y_leaf, late)
    else:
        if by_hops(axis_count(GROUP)):
            sources = sum_by_hops(kept, sent, GROUP, 1.0, False)
        else:
            sources = sum_over(join_halves(kept, sent, GROUP), GROUP)
        leaf = (y_leaf, sep_rows, leaf_upper, leaf_uinv)
        x_all, partial = solve_spread(at, sources, b_root, factors, leaf, bases)
    coefficients = sum_all(partial, EVERYONE, 1.0 / node_count, True)
    g_dense, c_dense = call(
        dense_kernel, [shape_of(extent, extent)] * 2, [block_cols, g_blocks, c_blocks], scalars=1
    )
    coef_out, cleaned, products = call(
        clean_kernel,
        [shape_of(ports, basis), shape_of(ports, extent + LANES), shape_of(2 * ports, LANES)],
        [coefficients, x_all, basis_leaf, basis_sep, basis_root, g_dense, c_dense],
        flops=14 * square,
    )
    parity = (lax.axis_index(EVERYONE) % 2).astype(jnp.int32).reshape(1)
    if by_hops(count):
        kept, sent = halves_of(products, EVERYONE)
        half = half_by_hops(kept, sent, EVERYONE, False) * (1.0 / node_count)
        pair = swap_pair(half, EVERYONE)
    else:
        sums = sum_over(products, EVERYONE, 1.0 / node_count)
        half, pair = halves_of(sums, EVERYONE)
    (inverse,) = call(factor_kernel, [shape_of(ports, ports)], [half])
    v_leaf, v_sep, v_root, g_out, c_out = call(
        finish_kernel,
        [
            shape_of(ports, extent),
            shape_of(sep_local, ports),
            shape_of(root_local, ports),
            shape_of(ports, ports),
            shape_of(ports, ports),
        ],
        [parity, half, pair, inverse, cleaned],
        scalars=1,
        flops=4 * square,
    )
    return (v_leaf.T, v_sep, v_root, coef_out.T, g_out, c_out)


def solution(mesh):
    rows = P(EVERYONE, None)
    columns = P(None, EVERYONE)
    return jax.shard_map(
        shards,
        mesh=mesh,
        in_specs=(rows,) * 10 + (columns,) + (rows,) * 9,
        out_specs=(rows, rows, rows, P(), P(), P()),
        check_vma=False,
    )
```

```python
import functools
import math

import jax
import jax.numpy as jnp
from jax import lax
from jax.experimental import pallas as pl
from jax.experimental.pallas import tpu as pltpu
from jax.sharding import PartitionSpec as P


LANES = 128
SUBLANES = 8
REPLICATE_BYTES = 4 << 20
VMEM_BYTES = 12 << 20
HOP_BITS = 2
HOP_DEVICES = 64
FIRST_UPWARD = True
EVERYONE = ("outer", "inner")
GROUP = ("inner",)
WHOLE = pl.BlockSpec(memory_space=pltpu.VMEM)
SCALAR = pl.BlockSpec(memory_space=pltpu.SMEM)


def contract(left, right, left_dim, right_dim, precision=lax.Precision.HIGHEST):
    return lax.dot_general(
        left,
        right,
        (((left_dim,), (right_dim,)), ((), ())),
        precision=precision,
        preferred_element_type=jnp.float32,
    )


def parts_of(value):
    high = value.astype(jnp.bfloat16)
    rest = value - high.astype(jnp.float32)
    middle = rest.astype(jnp.bfloat16)
    return high, middle, (rest - middle.astype(jnp.float32)).astype(jnp.bfloat16)


def dot_parts(left, right, right_dim):
    rows = left.shape[0]
    high, middle, low = parts_of(left)
    first, second, third = parts_of(right)
    three = contract(jnp.concatenate([high, middle, low], axis=0), first, 1, right_dim, None)
    two = contract(jnp.concatenate([high, middle], axis=0), second, 1, right_dim, None)
    one = contract(high, third, 1, right_dim, None)
    small = three[2 * rows :] + two[rows:] + one
    return three[:rows] + ((three[rows : 2 * rows] + two[:rows]) + small)


def dot_short(left, right, right_dim):
    rows = left.shape[0]
    high, middle, _ = parts_of(left)
    first, second, _ = parts_of(right)
    two = contract(jnp.concatenate([high, middle], axis=0), first, 1, right_dim, None)
    one = contract(high, second, 1, right_dim, None)
    return two[:rows] + (two[rows:] + one)


def dot_hot(left, hot, hot_dim):
    rows = left.shape[0]
    three = contract(
        jnp.concatenate(parts_of(left), axis=0),
        jnp.where(hot, 1.0, 0.0).astype(jnp.bfloat16),
        1,
        hot_dim,
        None,
    )
    return three[:rows] + (three[rows : 2 * rows] + three[2 * rows :])


def dot_nn(left, right):
    return dot_parts(left, right, 0)


def dot_nt(left, right):
    return dot_parts(left, right, 1)


def dot_tn(left, right):
    return contract(left, right, 0, 0)


def axis_count(axes):
    return math.prod(lax.axis_size(axis) for axis in axes)


def shape_of(*dims):
    return jax.ShapeDtypeStruct(dims, jnp.float32)


def call(body, outs, operands, far=(), scalars=0, flops=0, limit=VMEM_BYTES):
    specs = [SCALAR] * scalars + [WHOLE] * (len(operands) - scalars)
    specs += [pl.BlockSpec(memory_space=pltpu.HBM)] * len(far)
    operands = [*operands, *far]
    moved = sum(4 * operand.size for operand in operands) + sum(
        4 * math.prod(out.shape) for out in outs
    )
    scratch = [pltpu.VMEM(operand.shape, operand.dtype) for operand in far]
    if far:
        scratch.append(pltpu.SemaphoreType.DMA((len(far),)))
    return pl.pallas_call(
        body,
        out_shape=outs,
        in_specs=specs,
        out_specs=[WHOLE] * len(outs),
        scratch_shapes=scratch,
        compiler_params=pltpu.CompilerParams(vmem_limit_bytes=limit),
        cost_estimate=pl.CostEstimate(flops=flops, bytes_accessed=moved, transcendentals=0),
    )(*operands)


def fetch(far, copies, semaphores):
    moves = [
        pltpu.make_async_copy(source, target, semaphores.at[at])
        for at, (source, target) in enumerate(zip(far, copies))
    ]
    for move in moves:
        move.start()

    def read(at):
        moves[at].wait()
        return copies[at][...]

    return read


def iota(shape, dim):
    return lax.broadcasted_iota(jnp.int32, shape, dim)


def halves_up(wide):
    count = wide.shape[1] // LANES
    return jnp.concatenate(
        [wide[:, LANES * at : LANES * (at + 1)] for at in range(count)], axis=0
    )


def halves_down(tall, rows):
    count = tall.shape[0] // rows
    return jnp.concatenate([tall[rows * at : rows * (at + 1)] for at in range(count)], axis=1)


def exchange(blocks, axes):
    return lax.all_to_all(blocks, axes, 0, 0, tiled=True)


def gather_blocks(block, axes):
    count = axis_count(axes)
    return exchange(jnp.broadcast_to(block[None], (count,) + block.shape), axes)


def spread_kernel(scale, in_ref, out_ref):
    total = jnp.sum(in_ref[...], axis=0) * scale
    out_ref[...] = jnp.broadcast_to(total[None], out_ref.shape)


def sum_over(tall, axes, scale=1.0):
    count = axis_count(axes)
    size = tall.size
    depth = -(-size // (count * LANES))
    blocks = tall
    if size != count * depth * LANES:
        blocks = jnp.pad(tall.reshape(-1), (0, count * depth * LANES - size))
    blocks = blocks.reshape(count, depth, LANES)
    received = exchange(blocks, axes)
    (spread,) = call(
        functools.partial(spread_kernel, scale), [shape_of(count, depth, LANES)], [received]
    )
    whole = exchange(spread, axes)
    if size != count * depth * LANES:
        whole = whole.reshape(-1)[:size]
    return whole.reshape(tall.shape)


def is_power_of_two(count):
    return count & (count - 1) == 0


def hop(value, axes, low, width):
    count = axis_count(axes)
    total = value
    for pattern in range(1, 1 << width):
        pairs = [(source, source ^ (pattern << low)) for source in range(count)]
        total = total + lax.ppermute(value, axes, pairs)
    return total


def halves_of(tall, axes):
    half = tall.shape[0] // 2
    odd = lax.axis_index(axes) % 2 == 1
    kept = jnp.where(odd, tall[half:], tall[:half])
    return kept, jnp.where(odd, tall[:half], tall[half:])


def swap_pair(value, axes):
    count = axis_count(axes)
    return lax.ppermute(value, axes, [(source, source ^ 1) for source in range(count)])


def pair_up(mine, other, axes):
    odd = lax.axis_index(axes) % 2 == 1
    return jnp.concatenate([jnp.where(odd, other, mine), jnp.where(odd, mine, other)])


def half_by_hops(kept, sent, axes, upward):
    total = kept + swap_pair(sent, axes)
    spans = spans_of(axis_count(axes).bit_length() - 1)
    if upward:
        spans.reverse()
    for low, width in spans:
        total = hop(total, axes, low, width)
    return total


def sum_by_hops(kept, sent, axes, scale, upward):
    total = half_by_hops(kept, sent, axes, upward) * scale
    return pair_up(total, swap_pair(total, axes), axes)


def by_hops(count):
    return is_power_of_two(count) and 1 < count <= HOP_DEVICES


def swap_by_bits(blocks, position):
    size, bit = len(blocks), 0
    while 1 << bit < size:
        flip = ((position >> bit) & 1) == 1
        blocks = [
            jnp.where(flip, blocks[slot ^ (1 << bit)], blocks[slot]) for slot in range(size)
        ]
        bit += 1
    return blocks


def spans_of(bits):
    spans, low = [], bits
    while low > 1:
        width = min(HOP_BITS, low - 1)
        low -= width
        spans.append((low, width))
    return spans


def gather_rows(rows, axes):
    count = axis_count(axes)
    here = lax.axis_index(axes)
    held = rows
    places, size = [0], 1
    spans = spans_of(count.bit_length() - 1)
    for low, width in spans:
        blocks = [held]
        for pattern in range(1, 1 << width):
            pairs = [(source, source ^ (pattern << low)) for source in range(count)]
            blocks.append(lax.ppermute(held, axes, pairs))
        held = jnp.concatenate(swap_by_bits(blocks, here >> low))
        places = [digit * size + place for place in places for digit in range(1 << width)]
        size <<= width
    return held, swap_pair(held, axes), places


def leaf_kernel(count, at_ref, *refs):
    far, (y_ref, kept_ref, sent_ref, *packed_ref) = refs[:count], refs[count : -count - 1]
    read = fetch(far, refs[-count - 1 : -1], refs[-1])
    b_leaf, linv = read(0), read(1)
    y_leaf = dot_nt(b_leaf, linv)
    y_ref[...] = y_leaf
    contrib = dot_short(y_leaf, read(2), 1)
    rows = read(3)
    b_sep = read(4)
    extent = rows.shape[1]
    width = 2 * kept_ref.shape[0] // b_leaf.shape[0] * LANES
    hits = iota((width, extent), 0) == rows
    placed = dot_hot(contrib, hits, 1)
    own_rows = b_sep.shape[0]
    own = iota((own_rows, width), 1) == iota((own_rows, width), 0) + at_ref[0]
    tall = halves_up(dot_tn(b_sep, own.astype(jnp.float32)) - placed)
    half = kept_ref.shape[0]
    odd = (at_ref[0] // own_rows) % 2 == 1
    kept_ref[...] = jnp.where(odd, tall[half:], tall[:half])
    sent_ref[...] = jnp.where(odd, tall[:half], tall[half:])
    if packed_ref:
        pack_rows(at_ref[0], [read(at) for at in range(5, count)], packed_ref[0])


def pack_rows(at, values, out_ref):
    sep_l, sep_u, lower, upper, root_l, root_u, b_root = values
    rows, width = sep_l.shape
    own = iota((rows, width), 0) + at
    col = iota((rows, width), 1)

    def fold(lower, upper):
        diagonal = jnp.sum(jnp.where(col == own, lower, 0.0), axis=1, keepdims=True)
        return jnp.where(col < own, lower, upper), diagonal

    sep, sep_diagonal = fold(sep_l, sep_u)
    root, root_diagonal = fold(root_l, root_u)
    quarter = (LANES - b_root.shape[1]) // 2
    extra = jnp.concatenate(
        [
            b_root,
            jnp.broadcast_to(sep_diagonal, (rows, quarter)),
            jnp.broadcast_to(root_diagonal, (rows, quarter)),
        ],
        axis=1,
    )
    out_ref[...] = halves_up(jnp.concatenate([sep, lower, upper, root, extra], axis=1))


def fold_kernel(
    at_ref, y_ref, rows_ref, upper_ref, uinv_ref, q_ref, q_sep_ref, y_out_ref, carry_ref
):
    extent = y_ref.shape[1]
    width = carry_ref.shape[0]
    hits = (iota((width, extent), 0) == rows_ref[...]).astype(jnp.float32)
    carried = dot_nt(hits, upper_ref[...])
    both = jnp.concatenate([y_ref[...], carried], axis=0)
    solved = dot_short(both, uinv_ref[...], 1)
    projected = dot_short(solved, q_ref[...], 0)
    ports = y_ref.shape[0]
    y_out_ref[:, :extent] = solved[:ports]
    y_out_ref[:, extent:] = projected[:ports]
    carry_ref[:, :extent] = solved[ports:]
    carry_ref[:, extent:] = projected[ports:]
    own = pl.ds(pl.multiple_of(at_ref[0], SUBLANES), q_sep_ref.shape[0])
    carry_ref[own, extent:] = carry_ref[own, extent:] - q_sep_ref[...]


def solve_kernel(
    places,
    at_ref,
    half_ref,
    pair_ref,
    mine_ref,
    other_ref,
    y_ref,
    carry_ref,
    q_root_ref,
    x_sep_ref,
    root_ref,
    sent_ref,
):
    ports = y_ref.shape[0]
    own_rows = SUBLANES
    width = 2 * len(places) * own_rows
    tall = mine_ref.shape[0] // len(places)
    odd = (at_ref[0] // own_rows) % 2 == 1

    def ordered(mine, other):
        return jnp.where(odd, other, mine), jnp.where(odd, mine, other)

    def piece(first, size):
        strips = []
        for lane in range(first // LANES, (first + size) // LANES):
            blocks = []
            for place in places:
                start = place * tall + lane * own_rows
                rows = slice(start, start + own_rows)
                blocks.extend(ordered(mine_ref[rows], other_ref[rows]))
            strips.append(jnp.concatenate(blocks, axis=0))
        return jnp.concatenate(strips, axis=1)

    row = iota((width, width), 0)
    col = iota((width, width), 1)

    def unfold(folded, diagonal):
        lower = jnp.where(col < row, folded, jnp.where(col == row, diagonal, 0.0))
        return lower, jnp.where(col >= row, folded, 0.0)

    extra = piece(4 * width, LANES)
    quarter = (LANES - ports) // 2
    sep_l, sep_u = unfold(piece(0, width), extra[:, ports : ports + 1])
    root_l, root_u = unfold(
        piece(3 * width, width), extra[:, ports + quarter : ports + quarter + 1]
    )
    b_root = extra.T[:ports]
    sources = halves_down(jnp.concatenate(ordered(half_ref[...], pair_ref[...]), axis=0), ports)
    y_sep = dot_short(sources, sep_l, 1)
    y_root = dot_short(b_root - dot_short(y_sep, piece(width, width), 0), root_l, 1)
    x_root = dot_short(y_root, root_u, 1)
    x_sep = dot_short(y_sep - dot_short(x_root, piece(2 * width, width), 1), sep_u, 1)
    own = iota((LANES, width), 1) - at_ref[0] == iota((LANES, width), 0)
    own = own & (iota((LANES, width), 0) < own_rows)
    root_own = dot_hot(x_root, own, 1)[:, :own_rows]
    x_sep_ref[...] = x_sep
    root_ref[...] = dot_hot(x_root, own, 1)
    extent = y_ref.shape[1] - q_root_ref.shape[1]
    middle = extent + q_root_ref.shape[1] // 2

    def sent(ref):
        return jnp.where(odd, ref[:, extent:middle], ref[:, middle:])

    partial = sent(y_ref) - dot_nn(x_sep, sent(carry_ref))
    first = q_root_ref.shape[1] // 2
    q_root = jnp.where(odd, q_root_ref[:, :first], q_root_ref[:, first:])
    sent_ref[...] = halves_up(partial + dot_nn(root_own, q_root))


def rest_kernel(at_ref, x_sep_ref, root_ref, y_ref, carry_ref, q_root_ref, x_ref, kept_ref):
    ports, width = x_sep_ref.shape
    own_rows, basis = q_root_ref.shape
    odd = (at_ref[0] // own_rows) % 2 == 1
    extent = y_ref.shape[1] - basis
    middle = extent + basis // 2
    x_sep = x_sep_ref[...]
    root_own = root_ref[:, :own_rows]

    def wanted(ref):
        kept = jnp.where(odd, ref[:, middle:], ref[:, extent:middle])
        return jnp.concatenate([ref[:, :extent], kept], axis=1)

    folded = wanted(y_ref) - dot_nn(x_sep, wanted(carry_ref))
    q_root = jnp.where(odd, q_root_ref[:, basis // 2 :], q_root_ref[:, : basis // 2])
    kept_ref[...] = halves_up(folded[:, extent:] + dot_nn(root_own, q_root))
    x_ref[:, :extent] = folded[:, :extent]
    own = iota((LANES, width), 1) - at_ref[0] == iota((LANES, width), 0)
    own = own & (iota((LANES, width), 0) < own_rows)
    sep_own = dot_hot(x_sep, own, 1)[:, :own_rows]
    pad = jnp.zeros((ports, LANES - 2 * own_rows), jnp.float32)
    x_ref[:, extent:] = jnp.concatenate([sep_own, root_own, pad], axis=1)


def dense_kernel(at_ref, cols_ref, g_ref, c_ref, sent_ref, kept_ref):
    odd = at_ref[0] == 1
    block_rows, stored = cols_ref.shape
    size = g_ref.shape[1]
    for row in range(block_rows):
        for col in range(block_rows):
            totals = []
            for blocks_ref in (g_ref, c_ref):
                total = jnp.zeros((size, size), jnp.float32)
                for slot in range(stored):
                    start = (row * stored + slot) * size
                    block = blocks_ref[start : start + size, :]
                    total = total + jnp.where(cols_ref[row, slot] == col, block, 0.0)
                totals.append(total)
            rows = slice(size * row, size * (row + 1))
            lanes = slice(size * col, size * (col + 1))
            kept_ref[rows, lanes] = jnp.where(odd, totals[1], totals[0])
            sent_ref[rows, lanes] = jnp.where(odd, totals[0], totals[1])


def clean_kernel(
    coef_ref, x_ref, q_leaf_ref, q_sep_ref, q_root_ref, dense_ref, clean_out, out_ref
):
    ports, extent = x_ref.shape[0], q_leaf_ref.shape[0]
    coef = halves_down(coef_ref[...], ports)
    leaf = x_ref[:, :extent] - dot_nt(coef, q_leaf_ref[...])
    q_own = jnp.concatenate([q_sep_ref[...], q_root_ref[...]], axis=0)
    pad = LANES - q_own.shape[0]
    q_own = jnp.concatenate([q_own, jnp.zeros((pad, q_own.shape[1]), jnp.float32)], axis=0)
    own = x_ref[:, extent:] - dot_nt(coef, q_own)
    clean_out[:, :extent] = leaf
    clean_out[:, extent:] = own
    image = dot_short(leaf, dense_ref[...], 1)
    products = dot_short(leaf, jnp.concatenate([leaf, image], axis=0), 1)
    gram = products[:, :ports] + dot_short(own, own, 1)
    out_ref[...] = jnp.concatenate([gram, products[:, ports:]], axis=1)


def image_kernel(coef_ref, clean_ref, sent_ref, dense_ref, coef_out, out_ref):
    ports, extent = clean_ref.shape[0], dense_ref.shape[0]
    coef_out[...] = halves_down(coef_ref[...], ports)
    leaf = clean_ref[:, :extent]
    product = dot_short(leaf, dot_short(leaf, dense_ref[...], 1), 1)
    out_ref[...] = jnp.concatenate([sent_ref[:, :ports], product], axis=1)


def eliminate(tiles, offset, step):
    shape = tiles[0].shape
    rows = iota(shape, 0)
    tiles = list(tiles)

    def whole_row(tile, at):
        return jnp.broadcast_to(tile[at : at + 1, :], shape)

    def whole_col(tile, at):
        return jnp.broadcast_to(tile[:, at : at + 1], shape)

    for first in range(0, len(tiles) * SUBLANES, step):
        top, base = divmod(first, SUBLANES)
        pivots = [whole_row(tiles[top], base + t) for t in range(step)]
        columns = [
            [whole_col(tile, offset + first + t) for tile in tiles[top:]] for t in range(step)
        ]
        corner = [[whole_row(columns[u][0], base + t) for u in range(step)] for t in range(step)]
        factors = []
        for t in range(step):
            inverse = 1.0 / corner[t][t]
            for u in range(t + 1, step):
                ratio = corner[u][t] * inverse
                pivots[u] = pivots[u] - ratio * pivots[t]
                for v in range(t + 1, step):
                    corner[u][v] = corner[u][v] - ratio * corner[t][v]
            factor = [column * inverse for column in columns[t]]
            for v in range(t + 1, step):
                columns[v] = [c - f * corner[t][v] for c, f in zip(columns[v], factor)]
            factor[0] = jnp.where(rows > base + t, factor[0], 0.0)
            factors.append(factor)
        for at in range(top, len(tiles)):
            value = tiles[at]
            for t in range(step):
                value = value - factors[t][at - top] * pivots[t]
            tiles[at] = value
    return tiles


def factor_kernel(half_ref, inverse_ref):
    ports = inverse_ref.shape[0]
    diagonal = iota((ports, ports), 0) == iota((ports, ports), 1)
    joined = jnp.concatenate([jnp.where(diagonal, 1.0, 0.0), half_ref[:, :ports]], axis=1)
    tiles = [joined[at : at + SUBLANES] for at in range(0, ports, SUBLANES)]
    joined = jnp.concatenate(eliminate(tiles, ports, SUBLANES), axis=0)
    pivots = jnp.sum(jnp.where(diagonal, joined[:, ports:], 0.0), axis=1, keepdims=True)
    inverse = joined[:, :ports] / jnp.sqrt(pivots)
    inverse_ref[...] = inverse


def finish_kernel(
    at_ref, half_ref, pair_ref, inverse_ref, clean_ref, v_leaf_ref, v_sep_ref, v_root_ref, g_ref, c_ref
):
    ports = inverse_ref.shape[0]
    extent = v_leaf_ref.shape[1]
    own_rows = v_sep_ref.shape[0]
    inverse = inverse_ref[...]
    left = dot_short(
        inverse,
        jnp.concatenate([half_ref[:, ports:], pair_ref[:, ports:], clean_ref[...]], axis=1),
        0,
    )
    v_leaf_ref[...] = left[:, LANES : LANES + extent]
    own = left[:, LANES + extent :].T
    v_sep_ref[...] = own[:own_rows]
    v_root_ref[...] = own[own_rows : 2 * own_rows]
    left = jnp.concatenate([left[:, :ports], left[:, ports : 2 * ports]], axis=0)
    whole = dot_short(left, inverse, 1)
    odd = at_ref[0] == 1
    g_ref[...] = jnp.where(odd, whole[ports:], whole[:ports])
    c_ref[...] = jnp.where(odd, whole[:ports], whole[ports:])


def solve_replicated(at, kept, sent, packed, y_leaf, late):
    ports, extent = y_leaf.shape
    basis = late[-1].shape[1]
    rows, upper, uinv, q_leaf, q_sep, q_root = late
    width = 2 * kept.shape[0] // ports * LANES
    folded, carry = call(
        fold_kernel,
        [shape_of(ports, extent + basis), shape_of(width, extent + basis)],
        [at, y_leaf, rows, upper, uinv, q_leaf, q_sep],
        scalars=1,
        flops=30 * extent * extent * ports,
    )
    mine, other, places = gather_rows(packed, GROUP)
    half = half_by_hops(kept, sent, GROUP, FIRST_UPWARD)
    pair = swap_pair(half, GROUP)
    tall = basis // LANES // 2 * ports
    x_sep, x_root, sent = call(
        functools.partial(solve_kernel, places),
        [shape_of(ports, width), shape_of(ports, LANES), shape_of(tall, LANES)],
        [at, half, pair, mine, other, folded, carry, q_root],
        scalars=1,
        flops=22 * extent * extent * ports,
    )
    x_all, kept = call(
        rest_kernel,
        [shape_of(ports, extent + LANES), shape_of(tall, LANES)],
        [at, x_sep, x_root, folded, carry, q_root],
        scalars=1,
        flops=4 * extent * extent * ports,
    )
    return x_all, kept, sent


def solve_spread(at, sources, b_root, factors, leaf, bases):
    sep_linv, sep_uinv, sep_lower, sep_upper, root_linv, root_uinv = factors
    y_leaf, sep_rows, leaf_upper, leaf_uinv = leaf
    ports = y_leaf.shape[0]
    sep_local, sep_width = sep_linv.shape
    root_local, root_width = root_linv.shape
    row = iota((sep_local, sep_width), 0) + at[0]
    col = iota((sep_local, sep_width), 1)
    diagonal = jnp.sum(jnp.where(row == col, sep_linv, 0.0), axis=1, keepdims=True)
    folded = jnp.concatenate(
        [jnp.where(col < row, sep_linv, sep_uinv), jnp.broadcast_to(diagonal, (sep_local, LANES))],
        axis=1,
    )
    pair = gather_blocks(folded, GROUP).reshape(sep_width, -1)
    row = iota((sep_width, sep_width), 0)
    col = iota((sep_width, sep_width), 1)
    square = pair[:, :sep_width]
    sep_l = jnp.where(col < row, square, jnp.where(col == row, pair[:, sep_width:][:, :1], 0.0))
    sep_u = jnp.where(col >= row, square, 0.0)

    def own_rows(value):
        return lax.dynamic_slice(value, (at[0], 0), (sep_local, ports))

    y_sep = contract(sep_l, halves_down(sources, ports), 1, 1)
    count = axis_count(EVERYONE)
    update = contract(sep_lower, own_rows(y_sep), 1, 0).reshape(count, root_local, ports)
    held = b_root - exchange(update, EVERYONE).sum(axis=0)
    for factor in (root_linv, root_uinv):
        whole = gather_blocks(held, EVERYONE).reshape(root_width, ports)
        held = contract(factor, whole, 1, 0)
    x_root = held
    whole = gather_blocks(x_root, EVERYONE).reshape(root_width, ports)
    z_sep = own_rows(y_sep) - contract(sep_upper, whole, 1, 0)
    whole = gather_blocks(z_sep, GROUP).reshape(sep_width, ports)
    x_sep = contract(sep_u, whole, 1, 0)
    coupled = x_sep[sep_rows[0]]
    inner = y_leaf - contract(coupled, leaf_upper, 0, 1)
    x_leaf = contract(inner, leaf_uinv, 1, 1)
    own = jnp.concatenate([own_rows(x_sep), x_root], axis=0)
    partial = contract(x_leaf, bases[0], 1, 0) + contract(
        own, jnp.concatenate(bases[1:], axis=0), 0, 0
    )
    pad = jnp.zeros((ports, LANES - own.shape[0]), jnp.float32)
    halves = halves_of(halves_up(partial), EVERYONE)
    return jnp.concatenate([x_leaf, own.T, pad], axis=1), *halves


def shards(
    b_leaf,
    b_sep,
    b_root,
    leaf_linv,
    leaf_uinv,
    leaf_lower,
    leaf_upper,
    sep_rows,
    sep_linv,
    sep_uinv,
    sep_lower,
    sep_upper,
    root_linv,
    root_uinv,
    basis_leaf,
    basis_sep,
    basis_root,
    g_blocks,
    c_blocks,
    block_cols,
):
    extent, ports = b_leaf.shape
    sep_local = b_sep.shape[0]
    root_local = b_root.shape[0]
    sep_width = sep_linv.shape[1]
    basis = basis_leaf.shape[1]
    at = (lax.axis_index(GROUP) * sep_local).astype(jnp.int32).reshape(1)
    count = axis_count(EVERYONE)
    parity = (lax.axis_index(EVERYONE) % 2).astype(jnp.int32).reshape(1)
    node_count = float(count * (extent + sep_local + root_local))
    square = extent * extent * ports

    factors = (sep_linv, sep_uinv, sep_lower, sep_upper, root_linv, root_uinv)
    bases = (basis_leaf, basis_sep, basis_root)
    replicate = (
        count == axis_count(GROUP)
        and sep_local == root_local == SUBLANES
        and by_hops(count)
        and 4 * sep_width * (4 * sep_width + LANES) <= REPLICATE_BYTES
    )
    tall = sep_width // LANES * ports
    outs = [shape_of(ports, extent), shape_of(tall // 2, LANES), shape_of(tall // 2, LANES)]
    far = [b_leaf.T, leaf_linv, leaf_lower, sep_rows, b_sep]
    if replicate:
        outs.append(shape_of((4 * sep_width // LANES + 1) * sep_local, LANES))
        far += [sep_linv, sep_uinv, sep_lower.T, sep_upper, root_linv, root_uinv, b_root]
    y_leaf, kept, sent, *packed = call(
        functools.partial(leaf_kernel, len(far)),
        outs,
        [at],
        far=far,
        scalars=1,
        flops=6 * square,
        limit=None,
    )
    if replicate:
        late = [sep_rows, leaf_upper, leaf_uinv, *bases]
        x_all, kept, sent = solve_replicated(at, kept, sent, *packed, y_leaf, late)
    else:
        if by_hops(axis_count(GROUP)):
            sources = sum_by_hops(kept, sent, GROUP, 1.0, False)
        else:
            sources = sum_over(pair_up(kept, sent, GROUP), GROUP)
        leaf = (y_leaf, sep_rows, leaf_upper, leaf_uinv)
        x_all, kept, sent = solve_spread(at, sources, b_root, factors, leaf, bases)
    if by_hops(count):
        coefficients = sum_by_hops(kept, sent, EVERYONE, 1.0 / node_count, True)
    else:
        both = pair_up(kept, sent, EVERYONE)
        coefficients = sum_over(both, EVERYONE, 1.0 / node_count)
    sent_dense, kept_dense = call(
        dense_kernel,
        [shape_of(extent, extent)] * 2,
        [parity, block_cols, g_blocks, c_blocks],
        scalars=2,
    )
    cleaned, sent = call(
        clean_kernel,
        [shape_of(ports, extent + LANES), shape_of(ports, LANES)],
        [coefficients, x_all, basis_leaf, basis_sep, basis_root, sent_dense],
        flops=14 * square,
    )
    coef_out, kept = call(
        image_kernel,
        [shape_of(ports, basis), shape_of(ports, LANES)],
        [coefficients, cleaned, sent, kept_dense],
        flops=4 * square,
    )
    if by_hops(count):
        half = half_by_hops(kept, sent, EVERYONE, False) * (1.0 / node_count)
        pair = swap_pair(half, EVERYONE)
    else:
        sums = sum_over(pair_up(kept, sent, EVERYONE), EVERYONE, 1.0 / node_count)
        half, pair = halves_of(sums, EVERYONE)
    (inverse,) = call(factor_kernel, [shape_of(ports, ports)], [half])
    v_leaf, v_sep, v_root, g_out, c_out = call(
        finish_kernel,
        [
            shape_of(ports, extent),
            shape_of(sep_local, ports),
            shape_of(root_local, ports),
            shape_of(ports, ports),
            shape_of(ports, ports),
        ],
        [parity, half, pair, inverse, cleaned],
        scalars=1,
        flops=4 * square,
    )
    return (v_leaf.T, v_sep, v_root, coef_out.T, g_out, c_out)


def solution(mesh):
    rows = P(EVERYONE, None)
    columns = P(None, EVERYONE)
    return jax.shard_map(
        shards,
        mesh=mesh,
        in_specs=(rows,) * 10 + (columns,) + (rows,) * 9,
        out_specs=(rows, rows, rows, P(), P(), P()),
        check_vma=False,
    )
```
